256 devices in a mesh: ctx: 16 (over x, y), tp: 16 (over z, core).
Axes of the slice: x: 4, y: 4, z: 8, core: 2. Of those that a mesh axis runs over, the one named last changes fastest.
Arguments:
- query_rows: bfloat16 [16384, 8192], P('ctx', 'tp'), may hold values from -6 to 6
- key_rows: bfloat16 [16384, 8192], P('ctx', 'tp'), may hold values from -0.5 to 0.5
- value_rows: bfloat16 [16384, 8192], P('ctx', 'tp'), may hold values from -500 to 500
- gate_logits: bfloat16 [16384, 8192], P('ctx', 'tp'), may hold values from -6 to 6
- norm_gain: float32 [8192], P('tp'), may hold values from 0.1 to 1.9
- log_decay: float32 [64, 16384], P('tp', 'ctx'), may hold values from -3 to 0
- offsets: int32 [6], replicated, may hold values from 0 to 16383, as said below
- cotangent: bfloat16 [16384, 8192], P('ctx', 'tp'), may hold values from -6 to 6
Outputs:
- attended: bfloat16 [16384, 8192], P('ctx', 'tp')
- grad_query: bfloat16 [16384, 8192], P('ctx', 'tp')
- grad_key: bfloat16 [16384, 8192], P('ctx', 'tp')
- grad_value: bfloat16 [16384, 8192], P('ctx', 'tp')
- grad_gate: bfloat16 [16384, 8192], P('ctx', 'tp')
The draws below stay inside these ranges and needn't reach their ends.
Inputs may be any that keep to these rules, and one draw needn't show every extreme that they name: offsets[0] is 0 and the entries rise strictly; each is the first token of a rollout; every entry after the first lies among the last 1024 tokens of the 16384.
All inputs are finite; a program needn't handle non-finite values.
Results may differ from the reference program's by a relative error of at most 0.0035.
Values sent between devices are 32-bit elements; how exact they have to be, the bound alone decides.
No kernel may reach another device: no remote copies, remote signals or barrier semaphores. Data moves between devices by JAX's collectives and lax.ppermute only.
A program may use at most 128 MiB of HBM per device.

```python
import math
import jax
import jax.numpy as jnp
from jax import lax

D_HEAD = 128
HEAD_TOTAL = 64
TOK_DEV = 1024
TOKEN_TOTAL = 16384
BLOCK = 512
ROLLOUTS = 6


def draw_value_rows(key, part):
    key_base, key_row = jax.random.split(jax.random.fold_in(key, 11), 2)
    shape = (TOKEN_TOTAL, HEAD_TOTAL, D_HEAD)
    ladder = jnp.arange(HEAD_TOTAL, dtype=jnp.float32) / max(HEAD_TOTAL - 1, 1)
    head_scale = 3.0 ** ladder
    row_scale = jnp.exp(jax.random.uniform(key_row, (TOKEN_TOTAL, 1, 1), jnp.float32, 0.0, math.log(10.0)))
    base_value = jnp.clip(jax.random.normal(key_base, shape, jnp.float32), -6.0, 6.0)
    values = base_value * head_scale[None, :, None] * row_scale
    return values.reshape(TOKEN_TOTAL, HEAD_TOTAL * D_HEAD).astype(jnp.bfloat16)


def draw_log_decay(key, part):
    random_keys = jax.random.split(jax.random.fold_in(key, 23), 7)
    share = 0.5
    fast = jax.random.uniform(random_keys[0], (HEAD_TOTAL, 1), jnp.float32) < share
    fast_rate = 1.0 / jax.random.uniform(random_keys[1], (HEAD_TOTAL, 1), jnp.float32, 30.0, 50.0)
    slow_rate = jax.random.uniform(random_keys[2], (HEAD_TOTAL, 1), jnp.float32, 0.02, 0.12) / TOKEN_TOTAL
    base_value = jnp.where(fast, fast_rate, slow_rate)
    device_blocks = TOKEN_TOTAL // TOK_DEV
    log_two = math.log(2.0)
    device_share = jnp.exp(jax.random.uniform(random_keys[3], (HEAD_TOTAL, device_blocks, 1), jnp.float32, -log_two, log_two))
    device_share = jnp.broadcast_to(device_share, (HEAD_TOTAL, device_blocks, TOK_DEV)).reshape(HEAD_TOTAL, TOKEN_TOTAL)
    token_share = jnp.exp(jax.random.uniform(random_keys[4], (HEAD_TOTAL, TOKEN_TOTAL), jnp.float32, -log_two, log_two))
    surge_positions = jax.random.randint(random_keys[5], (HEAD_TOTAL, 2, 1), 0, TOKEN_TOTAL)
    surge_length = jax.random.uniform(random_keys[6], (HEAD_TOTAL, 2, 1), jnp.float32, math.log(0.5), math.log(0.8))
    chosen_positions = jnp.arange(TOKEN_TOTAL)[None, None, :]
    surge_groups = jnp.sum(jnp.where(chosen_positions == surge_positions, surge_length, 0.0), axis=1)
    return (-(base_value * device_share * token_share) + surge_groups).astype(jnp.float32)


def draw_offsets(key, part):
    lowest = TOKEN_TOTAL - TOK_DEV + 1
    picks = jax.random.permutation(jax.random.fold_in(key, 37), TOK_DEV - 1)[:ROLLOUTS - 1] + lowest
    return jnp.concatenate([jnp.zeros((1,), jnp.int32), jnp.sort(picks).astype(jnp.int32)])


def block_levels(own_key, extent, cuts, low, top_value):
    level, own = 1.0, jax.random.fold_in(own_key, 6)
    for axis_at, shards_of in cuts:
        heights = jnp.exp(jax.random.uniform(jax.random.fold_in(own, axis_at), (shards_of,), jnp.float32, low / len(cuts), top_value / len(cuts)))
        level = level * jnp.repeat(heights, extent[axis_at] // shards_of).reshape([-1 if axis == axis_at else 1 for axis in range(len(extent))])
    return level


def normal_values(stream_key, shape, scale, most, shards=(), held_as=jnp.bfloat16):
    values = jax.random.normal(stream_key, shape, jnp.float32) * scale
    if len(shards) > 0:
        values = block_levels(stream_key, shape, shards, -0.22, 0.18) * values
    return jnp.clip(values, min=-most, max=most).astype(held_as)


def setup_inputs(seed: int = 0) -> dict:
    key_of = jax.random.split(jax.random.key(seed), 9)
    return {
        "query_rows": normal_values(key_of[0], (TOKEN_TOTAL, HEAD_TOTAL * D_HEAD), 1.0, 6.0, ((0, 16), (1, 16))),
        "key_rows": normal_values(key_of[1], (TOKEN_TOTAL, HEAD_TOTAL * D_HEAD), D_HEAD ** -0.5, 0.5, ((0, 16), (1, 16))),
        "value_rows": draw_value_rows(jax.random.fold_in(key_of[8], 71), 0),
        "gate_logits": normal_values(key_of[3], (TOKEN_TOTAL, HEAD_TOTAL * D_HEAD), 1.5, 6.0, ((0, 16), (1, 16))),
        "norm_gain": jnp.clip(1.0 + 0.18 * jax.random.normal(key_of[4], (HEAD_TOTAL * D_HEAD,), jnp.float32), 0.1, 1.9),
        "log_decay": draw_log_decay(jax.random.fold_in(key_of[8], 71), 0),
        "offsets": draw_offsets(jax.random.fold_in(key_of[8], 71), 0),
        "cotangent": normal_values(key_of[7], (TOKEN_TOTAL, HEAD_TOTAL * D_HEAD), 1.0, 6.0, ((0, 16), (1, 16))),
    }


EPS_NORM = 1e-06
HIGHEST = lax.Precision.HIGHEST

def segment_ids(offsets, positions):
    hits = (offsets[None, :] <= positions[:, None]).astype(jnp.int32)
    return (lax.optimization_barrier(jnp.sum(hits, axis=1)) - 1).astype(jnp.int32)

def block_tables(decay_block, segment_block, segment_before):
    running = jnp.cumsum(decay_block)
    index_rows = jnp.arange(segment_block.shape[0])
    causal = (index_rows[None, :] <= index_rows[:, None]) & (segment_block[:, None] == segment_block[None, :])
    within = jnp.where(causal, jnp.exp(jnp.minimum(running[:, None] - running[None, :], 0.0)), 0.0)
    carry_weight = jnp.where(segment_block == segment_before, jnp.exp(running), 0.0)
    last_weight = jnp.where(segment_block == segment_block[-1], jnp.exp(jnp.minimum(running[-1] - running, 0.0)), 0.0)
    factor = jnp.where(segment_block[-1] == segment_before, jnp.exp(running[-1]), 0.0)
    return (within, carry_weight, last_weight, factor)

def head_forward(query_head, key_head, value_head, decay_head, segments, befores):

    def advance(carried, inputs):
        query_block, key_block, value_block, decay_block, segment_block, segment_before = inputs
        within, carry_weight, last_weight, factor = block_tables(decay_block, segment_block, segment_before)
        scores = jnp.dot(query_block, key_block.T, preferred_element_type=jnp.float32)
        weights = (scores * within).astype(jnp.bfloat16)
        query_f = query_block.astype(jnp.float32)
        key_f = key_block.astype(jnp.float32)
        value_f = value_block.astype(jnp.float32)
        output = jnp.dot(weights, value_block, preferred_element_type=jnp.float32) + carry_weight[:, None] * jnp.dot(query_f, carried, precision=HIGHEST)
        updated = factor * carried + jnp.dot((key_f * last_weight[:, None]).T, value_f, precision=HIGHEST)
        return (updated, (output, carried))
    initial = jnp.zeros((D_HEAD, D_HEAD), jnp.float32)
    _, (outputs, states) = lax.scan(advance, initial, (query_head, key_head, value_head, decay_head, segments, befores))
    return (outputs, states)

def head_backward(query_head, key_head, value_head, decay_head, segments, befores, states, grad_head):

    def retreat(coming, inputs):
        query_block, key_block, value_block, decay_block, segment_block, segment_before, state_block, grad_block = inputs
        within, carry_weight, last_weight, factor = block_tables(decay_block, segment_block, segment_before)
        scores = jnp.dot(query_block, key_block.T, preferred_element_type=jnp.float32)
        weights = (scores * within).astype(jnp.bfloat16)
        grad_low = grad_block.astype(jnp.bfloat16)
        query_f = query_block.astype(jnp.float32)
        key_f = key_block.astype(jnp.float32)
        value_f = value_block.astype(jnp.float32)
        back_scores = (jnp.dot(grad_low, value_block.T, preferred_element_type=jnp.float32) * within).astype(jnp.bfloat16)
        grad_q = jnp.dot(back_scores, key_block, preferred_element_type=jnp.float32) + carry_weight[:, None] * jnp.dot(grad_block, state_block.T, precision=HIGHEST)
        grad_k = jnp.dot(back_scores.T, query_block, preferred_element_type=jnp.float32) + last_weight[:, None] * jnp.dot(value_f, coming.T, precision=HIGHEST)
        grad_v = jnp.dot(weights.T, grad_low, preferred_element_type=jnp.float32) + last_weight[:, None] * jnp.dot(key_f, coming, precision=HIGHEST)
        earlier = factor * coming + jnp.dot((query_f * carry_weight[:, None]).T, grad_block, precision=HIGHEST)
        return (earlier, (grad_q, grad_k, grad_v))
    initial = jnp.zeros((D_HEAD, D_HEAD), jnp.float32)
    _, grads = lax.scan(retreat, initial, (query_head, key_head, value_head, decay_head, segments, befores, states, grad_head), reverse=True)
    return grads

def reference(query_rows, key_rows, value_rows, gate_logits, norm_gain, log_decay, offsets, cotangent):
    head_count = log_decay.shape[0]
    token_count = query_rows.shape[0]
    block_count = token_count // BLOCK
    feature_total = head_count * D_HEAD
    positions = jnp.arange(token_count, dtype=jnp.int32)
    segments = segment_ids(offsets, positions).reshape(block_count, BLOCK)
    starts = positions.reshape(block_count, BLOCK)[:, 0]
    befores = segment_ids(offsets, (starts - 1).astype(jnp.int32))

    def to_heads(array):
        return array.reshape(block_count, BLOCK, head_count, D_HEAD).transpose(2, 0, 1, 3)

    def from_heads(array):
        return array.transpose(1, 2, 0, 3).reshape(token_count, feature_total).astype(jnp.bfloat16)
    queries = to_heads(query_rows)
    key_heads = to_heads(key_rows)
    value_heads = to_heads(value_rows)
    decays = log_decay.reshape(head_count, block_count, BLOCK)

    def forward_one(inputs):
        return head_forward(inputs[0], inputs[1], inputs[2], inputs[3], segments, befores)
    attention, states = lax.map(forward_one, (queries, key_heads, value_heads, decays))
    squares = lax.optimization_barrier(jnp.sum(attention * attention, axis=(0, 3)))
    rms = jnp.sqrt(squares / feature_total + EPS_NORM)[None, :, :, None]
    normed = attention / rms
    gain_heads = norm_gain.reshape(head_count, 1, 1, D_HEAD)
    gate_sig = jax.nn.sigmoid(to_heads(gate_logits).astype(jnp.float32))
    attended = normed * gain_heads * gate_sig
    upstream = to_heads(cotangent).astype(jnp.float32)
    grad_gate = upstream * normed * gain_heads * gate_sig * (1.0 - gate_sig)
    grad_normed = upstream * gain_heads * gate_sig
    inner = lax.optimization_barrier(jnp.sum(grad_normed * normed, axis=(0, 3)))[None, :, :, None]
    grad_attn = (grad_normed - normed * (inner / feature_total)) / rms

    def backward_one(inputs):
        return head_backward(inputs[0], inputs[1], inputs[2], inputs[3], segments, befores, inputs[4], inputs[5])
    grad_query, grad_key, grad_value = lax.map(backward_one, (queries, key_heads, value_heads, decays, states, grad_attn))
    return (from_heads(attended), from_heads(grad_query), from_heads(grad_key), from_heads(grad_value), from_heads(grad_gate))
```

```python
import functools

import jax
import jax.numpy as jnp
from jax import lax
from jax.experimental import pallas as pl
from jax.experimental.pallas import tpu as pltpu
from jax.sharding import PartitionSpec as P

D_HEAD = 128
BLOCK = 512
TILE = 256
CHUNK = 128
EPS_NORM = 1e-06
RESET = -128.0
NEVER = -1e30
F32 = jnp.float32
BF16 = jnp.bfloat16
PAD = 8


def nn(a, b):
    return lax.dot_general(a, b, (((1,), (0,)), ((), ())), preferred_element_type=F32)


def nt(a, b):
    return lax.dot_general(a, b, (((1,), (1,)), ((), ())), preferred_element_type=F32)


def tn(a, b):
    return lax.dot_general(a, b, (((0,), (0,)), ((), ())), preferred_element_type=F32)


def split(x):
    high = x.astype(BF16)
    return high, (x - high.astype(F32)).astype(BF16)


def halves(x):
    return x[:, :D_HEAD] + x[:, D_HEAD:]


def column(row):
    return jnp.broadcast_to(row, (CHUNK, row.shape[1])).T


def triangle(rows_are_later):
    first = lax.broadcasted_iota(jnp.int32, (TILE, TILE), 0)
    second = lax.broadcasted_iota(jnp.int32, (TILE, TILE), 1)
    return first >= second if rows_are_later else first <= second


def state_of(rows, weighted):
    high, low = split(weighted)
    return halves(tn(rows, jnp.concatenate([high, low], axis=1)))


def tables_kernel(heads, offsets_ref, decay_ref, key_ref, value_ref, table_ref, send_ref, first_ref):
    head = pl.program_id(0)

    @pl.when(head == 0)
    def _():
        decay = decay_ref[...]
        blocks = decay.shape[1] // BLOCK
        running = jnp.concatenate(
            [decay[:, b * BLOCK : (b + 1) * BLOCK] for b in range(blocks)], axis=0
        )
        lane = lax.broadcasted_iota(jnp.int32, running.shape, 1)
        row = lax.broadcasted_iota(jnp.int32, running.shape, 0)
        position = lax.axis_index("ctx") * decay.shape[1] + (row // heads) * BLOCK + lane
        starts = position == offsets_ref[0]
        for index in range(1, offsets_ref.shape[0]):
            starts = starts | (position == offsets_ref[index])
        running = jnp.where(starts, running + RESET, running)
        step = 1
        while step < BLOCK:
            running = running + jnp.where(lane >= step, pltpu.roll(running, step, axis=1), 0.0)
            step *= 2
        last = jnp.broadcast_to(running[:, BLOCK - 1 :], running.shape)
        table_ref[0] = running
        table_ref[1] = jnp.exp(running)
        table_ref[2] = jnp.exp(jnp.minimum(last - running, 0.0))
        table_ref[3] = jnp.exp(last)

    states = []
    factors = []
    for b in range(2):
        at = pl.ds(b * heads + head, 1)
        tokens = pl.ds(b * BLOCK, BLOCK)
        weighted = value_ref[tokens, :].astype(F32) * column(table_ref[2, at, :])
        states.append(state_of(key_ref[tokens, :], weighted))
        factors.append(table_ref[3, at, :][:, :D_HEAD])
    first_ref[0] = states[0]
    total = factors[1] * states[0] + states[1]
    both = jnp.broadcast_to(factors[0] * factors[1], (PAD, D_HEAD))
    rows = send_ref.shape[1] - PAD
    for part in range(send_ref.shape[0]):
        send_ref[part, :rows, :] = total[part * rows : (part + 1) * rows]
        send_ref[part, rows:, :] = both


def scan_kernel(backward, got_ref, out_ref):
    count, rows, _ = out_ref.shape
    carried = jnp.zeros(out_ref.shape[1:], F32)
    for step in range(count):
        source = count - 1 - step if backward else step
        out_ref[source] = carried
        carried = got_ref[source, rows : rows + 1, :] * carried + got_ref[source, :rows, :]


def inner_kernel(heads, query_ref, key_ref, value_ref, table_ref, out_ref):
    head = pl.program_id(0)
    causal = triangle(True)
    for b in range(2):
        row = table_ref[0, pl.ds(b * heads + head, 1), :]
        col = column(row)
        for t in range(BLOCK // TILE):
            later = pl.ds(b * BLOCK + t * TILE, TILE)
            earlier = pl.ds(b * BLOCK, (t + 1) * TILE)
            mine = col[t * TILE : (t + 1) * TILE]
            mine = jnp.concatenate([mine, mine], axis=1)
            pieces = []
            for s in range(t + 1):
                gap = mine - row[:, s * TILE : (s + 1) * TILE]
                if s == t:
                    gap = jnp.where(causal, gap, NEVER)
                pieces.append(jnp.exp(gap))
            within = pieces[0] if t == 0 else jnp.concatenate(pieces, axis=1)
            scores = nt(query_ref[later, :], key_ref[earlier, :])
            weights = (scores * within).astype(BF16)
            out_ref[later, :] = nn(weights, value_ref[earlier, :])


def gate_kernel(gate_ref, cotangent_ref, gain_ref, out_ref):
    signal = jax.nn.sigmoid(gate_ref[...].astype(F32))
    out_ref[...] = cotangent_ref[...].astype(F32) * gain_ref[...] * signal


def attention_kernel(
    heads, query_ref, inner_ref, before_ref, first_ref, table_ref, normgrad_ref, out_ref, send_ref, squares, products
):
    head = pl.program_id(0)

    @pl.when(head == 0)
    def _():
        squares[...] = jnp.zeros_like(squares)
        products[...] = jnp.zeros_like(products)

    state = before_ref[0]
    for b in range(2):
        at = pl.ds(b * heads + head, 1)
        tokens = pl.ds(b * BLOCK, BLOCK)
        if b == 1:
            factor = table_ref[3, pl.ds(head, 1), :][:, :D_HEAD]
            state = factor * state + first_ref[0]
        far = halves(nn(query_ref[tokens, :], jnp.concatenate(split(state), axis=1)))
        attention = inner_ref[tokens, :] + column(table_ref[1, at, :]) * far
        out_ref[tokens, :] = attention
        squares[tokens, :] += attention * attention
        products[tokens, :] += attention * normgrad_ref[tokens, :]

    @pl.when(head == heads - 1)
    def _():
        rows = []
        for sums in (squares, products):
            for chunk in range(sums.shape[0] // CHUNK):
                part = sums[pl.ds(chunk * CHUNK, CHUNK), :]
                rows.append(jnp.sum(part.T, axis=0, keepdims=True))
        stats = jnp.concatenate(rows, axis=0)
        send_ref[...] = jnp.broadcast_to(stats[None], send_ref.shape)


def gradient_kernel(
    heads,
    features,
    got_ref,
    attention_ref,
    normgrad_ref,
    query_ref,
    table_ref,
    grad_ref,
    inverse_ref,
    send_ref,
    second_ref,
    slope,
):
    head = pl.program_id(0)

    @pl.when(head == 0)
    def _():
        stats = got_ref[0]
        for source in range(1, got_ref.shape[0]):
            stats = stats + got_ref[source]
        chunks = stats.shape[0] // 2
        inverse = 1.0 / jnp.sqrt(stats[:chunks] / features + EPS_NORM)
        inner = stats[chunks:] * inverse / features
        for chunk in range(chunks):
            tokens = pl.ds(chunk * CHUNK, CHUNK)
            inverse_ref[tokens, :] = column(inverse[chunk : chunk + 1])
            slope[tokens, :] = column(inner[chunk : chunk + 1])

    states = []
    factors = []
    for b in range(2):
        at = pl.ds(b * heads + head, 1)
        tokens = pl.ds(b * BLOCK, BLOCK)
        inverse = inverse_ref[tokens, :]
        normed = attention_ref[tokens, :] * inverse
        grad = (normgrad_ref[tokens, :] - normed * slope[tokens, :]) * inverse
        grad_ref[tokens, :] = grad
        states.append(state_of(query_ref[tokens, :], grad * column(table_ref[1, at, :])))
        factors.append(table_ref[3, at, :][:, :D_HEAD])
    second_ref[0] = states[1]
    total = factors[0] * states[1] + states[0]
    both = jnp.broadcast_to(factors[0] * factors[1], (PAD, D_HEAD))
    rows = send_ref.shape[1] - PAD
    for part in range(send_ref.shape[0]):
        send_ref[part, :rows, :] = total[part * rows : (part + 1) * rows]
        send_ref[part, rows:, :] = both


def back_kernel(
    heads,
    query_ref,
    key_ref,
    value_ref,
    grad_ref,
    before_ref,
    first_ref,
    table_ref,
    gquery_ref,
    gkey_ref,
    gvalue_ref,
):
    head = pl.program_id(0)
    causal = triangle(False)
    state = before_ref[0]
    for b in range(2):
        at = pl.ds(b * heads + head, 1)
        if b == 1:
            factor = table_ref[3, pl.ds(head, 1), :][:, :D_HEAD]
            state = factor * state + first_ref[0]
        row = table_ref[0, at, :]
        col = column(row)
        block = pl.ds(b * BLOCK, BLOCK)
        grad, rest = split(grad_ref[block, :])
        state_high, state_low = split(state)
        far = halves(nt(grad, jnp.concatenate([state_high, state_low], axis=0))) + nt(rest, state_high)
        gquery = [None] * (BLOCK // TILE)
        for s in range(BLOCK // TILE):
            start = s * TILE
            earlier = pl.ds(b * BLOCK + start, TILE)
            later = pl.ds(b * BLOCK + start, BLOCK - start)
            mine = col[start : start + TILE]
            mine = jnp.concatenate([mine, mine], axis=1)
            pieces = []
            for t in range(s, BLOCK // TILE):
                gap = row[:, t * TILE : (t + 1) * TILE] - mine
                if s == t:
                    gap = jnp.where(causal, gap, NEVER)
                pieces.append(jnp.exp(gap))
            within = pieces[0] if len(pieces) == 1 else jnp.concatenate(pieces, axis=1)
            key_tile = key_ref[earlier, :]
            queries = query_ref[later, :]
            grads = grad[start:]
            weights = (nt(key_tile, queries) * within).astype(BF16)
            backs = (nt(value_ref[earlier, :], grads) * within).astype(BF16)
            gkey_ref[earlier, :] = nn(backs, queries)
            gvalue_ref[earlier, :] = nn(weights, grads)
            part = tn(backs, key_tile)
            for t in range(s, BLOCK // TILE):
                piece = part[(t - s) * TILE : (t - s + 1) * TILE]
                gquery[t] = piece if gquery[t] is None else gquery[t] + piece
        total = jnp.concatenate(gquery, axis=0) + column(table_ref[1, at, :]) * far
        gquery_ref[block, :] = total.astype(BF16)


def output_kernel(attention_ref, inverse_ref, normgrad_ref, gate_ref, gain_ref, attended_ref, ggate_ref):
    normed = attention_ref[...] * inverse_ref[...]
    signal = jax.nn.sigmoid(gate_ref[...].astype(F32))
    attended_ref[...] = (normed * gain_ref[...] * signal).astype(BF16)
    ggate_ref[...] = (normgrad_ref[...] * normed * (1.0 - signal)).astype(BF16)


def far_kernel(
    heads, key_ref, value_ref, ikey_ref, ivalue_ref, after_ref, second_ref, table_ref, gkey_ref, gvalue_ref
):
    head = pl.program_id(0)
    state = after_ref[0]
    for b in (1, 0):
        at = pl.ds(b * heads + head, 1)
        tokens = pl.ds(b * BLOCK, BLOCK)
        if b == 0:
            factor = table_ref[3, pl.ds(heads + head, 1), :][:, :D_HEAD]
            state = factor * state + second_ref[0]
        high, low = split(state)
        weight = column(table_ref[2, at, :])
        far_key = halves(nt(value_ref[tokens, :], jnp.concatenate([high, low], axis=0)))
        far_value = halves(nn(key_ref[tokens, :], jnp.concatenate([high, low], axis=1)))
        gkey_ref[tokens, :] = (ikey_ref[tokens, :] + weight * far_key).astype(BF16)
        gvalue_ref[tokens, :] = (ivalue_ref[tokens, :] + weight * far_value).astype(BF16)


def local(query_rows, key_rows, value_rows, gate_logits, norm_gain, log_decay, offsets, cotangent):
    heads = log_decay.shape[0]
    tokens, width = query_rows.shape
    ctx, tp = lax.axis_size("ctx"), lax.axis_size("tp")
    features = float(tp * width)
    gain = norm_gain.reshape(1, width)
    slice_rows = heads * D_HEAD // ctx
    parts = ctx // heads
    stat_rows = 2 * tokens // CHUNK

    per_head = pl.BlockSpec((tokens, D_HEAD), lambda h: (0, h))
    per_gain = pl.BlockSpec((1, D_HEAD), lambda h: (0, h))
    per_state = pl.BlockSpec((1, D_HEAD, D_HEAD), lambda h: (h, 0, 0))
    per_send = pl.BlockSpec((parts, slice_rows + PAD, D_HEAD), lambda h: (h, 0, 0))
    table_spec = pl.BlockSpec((4, 2 * heads, BLOCK), lambda h: (0, 0, 0))
    stat_spec = pl.BlockSpec((tp, stat_rows, CHUNK), lambda h: (0, 0, 0))
    column_spec = pl.BlockSpec((tokens, CHUNK), lambda h: (0, 0))

    def rows(dtype):
        return jax.ShapeDtypeStruct((tokens, width), dtype)

    states = jax.ShapeDtypeStruct((heads, D_HEAD, D_HEAD), F32)
    sends = jax.ShapeDtypeStruct((ctx, slice_rows + PAD, D_HEAD), F32)
    slices = jax.ShapeDtypeStruct((ctx, slice_rows, D_HEAD), F32)
    table = jax.ShapeDtypeStruct((4, 2 * heads, BLOCK), F32)

    def call(body, name, in_specs, out_specs, out_shape, scratch=(), flops=0, moved=0, grid=True):
        return pl.pallas_call(
            body,
            grid=(heads,) if grid else (),
            in_specs=in_specs,
            out_specs=out_specs,
            out_shape=out_shape,
            scratch_shapes=scratch,
            name=name,
            cost_estimate=pl.CostEstimate(
                flops=flops, bytes_accessed=moved, transcendentals=tokens * width
            ),
            compiler_params=pltpu.CompilerParams(vmem_limit_bytes=24 << 20),
        )

    size = tokens * width
    quad = 2 * size * BLOCK
    near = 2 * size * D_HEAD

    table_values, send, first = call(
        functools.partial(tables_kernel, heads),
        "tables",
        [pl.BlockSpec(memory_space=pltpu.SMEM), pl.BlockSpec((heads, tokens), lambda h: (0, 0)), per_head, per_head],
        (table_spec, per_send, per_state),
        (table, sends, states),
        flops=2 * near,
        moved=4 * size,
    )(offsets, log_decay, key_rows, value_rows)

    def scan(backward, got):
        whole = pl.BlockSpec(memory_space=pltpu.VMEM)
        return call(
            functools.partial(scan_kernel, backward), "scan", [whole], whole, slices, moved=8 * slices.size, grid=False
        )(got)

    def exchange(values, axis):
        return lax.all_to_all(values, axis, 0, 0, tiled=True)

    got = exchange(send, "ctx")
    inner = call(
        functools.partial(inner_kernel, heads),
        "inner",
        [per_head] * 3 + [table_spec],
        per_head,
        rows(F32),
        flops=2 * quad,
        moved=10 * size,
    )(query_rows, key_rows, value_rows, table_values)
    before = exchange(scan(False, got), "ctx").reshape(heads, D_HEAD, D_HEAD)
    normgrad = call(
        gate_kernel,
        "gate",
        [per_head, per_head, per_gain],
        per_head,
        rows(F32),
        flops=8 * size,
        moved=8 * size,
    )(gate_logits, cotangent, gain)

    attention, stats = call(
        functools.partial(attention_kernel, heads),
        "attention",
        [per_head, per_head, per_state, per_state, table_spec, per_head],
        (per_head, stat_spec),
        (rows(F32), jax.ShapeDtypeStruct((tp, stat_rows, CHUNK), F32)),
        scratch=[pltpu.VMEM((tokens, D_HEAD), F32)] * 2,
        flops=2 * near,
        moved=14 * size,
    )(query_rows, inner, before, first, table_values, normgrad)
    stats = exchange(stats, "tp")

    grad, inverse, send, second = call(
        functools.partial(gradient_kernel, heads, features),
        "gradient",
        [stat_spec, per_head, per_head, per_head, table_spec],
        (per_head, column_spec, per_send, per_state),
        (rows(F32), jax.ShapeDtypeStruct((tokens, CHUNK), F32), sends, states),
        scratch=[pltpu.VMEM((tokens, CHUNK), F32)],
        flops=2 * near,
        moved=14 * size,
    )(stats, attention, normgrad, query_rows, table_values)
    got = exchange(send, "ctx")
    grad_query, inner_key, inner_value = call(
        functools.partial(back_kernel, heads),
        "back",
        [per_head] * 4 + [per_state, per_state, table_spec],
        (per_head, per_head, per_head),
        (rows(BF16), rows(F32), rows(F32)),
        flops=5 * quad,
        moved=20 * size,
    )(query_rows, key_rows, value_rows, grad, before, first, table_values)
    after = exchange(scan(True, got), "ctx").reshape(heads, D_HEAD, D_HEAD)
    attended, grad_gate = call(
        output_kernel,
        "output",
        [per_head, column_spec, per_head, per_head, per_gain],
        (per_head, per_head),
        (rows(BF16), rows(BF16)),
        flops=12 * size,
        moved=14 * size,
    )(attention, inverse, normgrad, gate_logits, gain)
    grad_key, grad_value = call(
        functools.partial(far_kernel, heads),
        "far",
        [per_head] * 4 + [per_state, per_state, table_spec],
        (per_head, per_head),
        (rows(BF16), rows(BF16)),
        flops=4 * near,
        moved=16 * size,
    )(key_rows, value_rows, inner_key, inner_value, after, second, table_values)
    return (attended, grad_query, grad_key, grad_value, grad_gate)


def solution(mesh):
    placed = (
        P("ctx", "tp"),
        P("ctx", "tp"),
        P("ctx", "tp"),
        P("ctx", "tp"),
        P("tp"),
        P("tp", "ctx"),
        P(),
        P("ctx", "tp"),
    )
    return jax.shard_map(
        local,
        mesh=mesh,
        in_specs=placed,
        out_specs=(P("ctx", "tp"), P("ctx", "tp"), P("ctx", "tp"), P("ctx", "tp"), P("ctx", "tp")),
        check_vma=False,
    )
```

```python
import functools

import jax
import jax.numpy as jnp
from jax import lax
from jax.experimental import pallas as pl
from jax.experimental.pallas import tpu as pltpu
from jax.sharding import PartitionSpec as P

D_HEAD = 128
BLOCK = 512
TILE = 256
CHUNK = 128
EPS_NORM = 1e-06
RESET = -128.0
NEVER = -1e30
F32 = jnp.float32
BF16 = jnp.bfloat16
PAD = 8
ROOM = 24 << 20


def nn(a, b):
    return lax.dot_general(a, b, (((1,), (0,)), ((), ())), preferred_element_type=F32)


def nt(a, b):
    return lax.dot_general(a, b, (((1,), (1,)), ((), ())), preferred_element_type=F32)


def tn(a, b):
    return lax.dot_general(a, b, (((0,), (0,)), ((), ())), preferred_element_type=F32)


def split(x):
    high = x.astype(BF16)
    return high, (x - high.astype(F32)).astype(BF16)


def halves(x):
    return x[:, :D_HEAD] + x[:, D_HEAD:]


def column(row):
    return jnp.broadcast_to(row, (CHUNK, row.shape[1])).T


def triangle(rows_are_later):
    first = lax.broadcasted_iota(jnp.int32, (TILE, TILE), 0)
    second = lax.broadcasted_iota(jnp.int32, (TILE, TILE), 1)
    return first >= second if rows_are_later else first <= second


def state_of(rows, weighted):
    high, low = split(weighted)
    return halves(tn(rows, jnp.concatenate([high, low], axis=1)))


def lanes(head):
    return slice(head * D_HEAD, (head + 1) * D_HEAD)


def rows_of(block):
    return slice(block * BLOCK, (block + 1) * BLOCK)


def pair(tile):
    return jnp.concatenate([tile, tile], axis=1)


def put_slices(send_ref, head, heads, total, factor):
    parts = send_ref.shape[0] // heads
    rows = send_ref.shape[1] - PAD
    both = jnp.broadcast_to(factor, (PAD, D_HEAD))
    for part in range(parts):
        send_ref[head * parts + part, :rows, :] = total[part * rows : (part + 1) * rows]
        send_ref[head * parts + part, rows:, :] = both


def factor_of(table_ref, block, heads, head):
    at = block * heads + head
    return table_ref[3, at : at + 1, :D_HEAD]


def tables_kernel(
    heads,
    offsets_hbm,
    decay_hbm,
    key_hbm,
    value_hbm,
    table_ref,
    send_ref,
    first_hbm,
    key_ref,
    value_ref,
    first_ref,
    decay_ref,
    offsets_ref,
    sems,
):
    loads = [
        pltpu.make_async_copy(offsets_hbm, offsets_ref, sems.at[0]),
        pltpu.make_async_copy(decay_hbm, decay_ref, sems.at[1]),
    ]
    for block in range(2):
        at = pl.ds(block * BLOCK, BLOCK)
        for source, target in ((key_hbm, key_ref), (value_hbm, value_ref)):
            loads.append(pltpu.make_async_copy(source.at[at], target.at[at], sems.at[len(loads)]))
    for load in loads:
        load.start()
    loads[0].wait()
    loads[1].wait()
    decay = decay_ref[...]
    running = jnp.concatenate([decay[:, :BLOCK], decay[:, BLOCK:]], axis=0)
    lane = lax.broadcasted_iota(jnp.int32, running.shape, 1)
    row = lax.broadcasted_iota(jnp.int32, running.shape, 0)
    position = lax.axis_index("ctx") * decay.shape[1] + (row // heads) * BLOCK + lane
    starts = position == offsets_ref[0]
    for index in range(1, offsets_ref.shape[0]):
        starts = starts | (position == offsets_ref[index])
    running = jnp.where(starts, running + RESET, running)
    step = 1
    while step < BLOCK:
        running = running + jnp.where(lane >= step, pltpu.roll(running, step, axis=1), 0.0)
        step *= 2
    last = jnp.broadcast_to(running[:, BLOCK - 1 :], running.shape)
    until_last = jnp.exp(jnp.minimum(last - running, 0.0))
    table_ref[0] = running
    table_ref[1] = jnp.exp(running)
    table_ref[2] = until_last
    table_ref[3] = jnp.exp(last)
    for block in range(2):
        loads[2 + 2 * block].wait()
        loads[3 + 2 * block].wait()
        tokens = rows_of(block)
        for head in range(heads):
            at = block * heads + head
            weighted = value_ref[tokens, lanes(head)].astype(F32) * column(until_last[at : at + 1])
            state = state_of(key_ref[tokens, lanes(head)], weighted)
            if block == 0:
                first_ref[head] = state
            else:
                factor = factor_of(table_ref, 1, heads, head)
                put_slices(
                    send_ref,
                    head,
                    heads,
                    factor * first_ref[head] + state,
                    factor * factor_of(table_ref, 0, heads, head),
                )
        if block == 0:
            store = pltpu.make_async_copy(first_ref, first_hbm, sems.at[len(loads)])
            store.start()
    store.wait()


def scan_kernel(backward, got_ref, _, out_ref):
    count, rows, _ = out_ref.shape
    carried = jnp.zeros(out_ref.shape[1:], F32)
    for step in range(count):
        source = count - 1 - step if backward else step
        out_ref[source] = carried
        carried = got_ref[source, rows : rows + 1, :] * carried + got_ref[source, :rows, :]


def inner_kernel(heads, query_hbm, key_hbm, value_hbm, table_ref, out_ref, query_ref, key_ref, value_ref, sems):
    loads = []
    for block in range(2):
        at = pl.ds(block * BLOCK, BLOCK)
        for source, target in ((query_hbm, query_ref), (key_hbm, key_ref), (value_hbm, value_ref)):
            loads.append(pltpu.make_async_copy(source.at[at], target.at[at], sems.at[len(loads)]))
            loads[-1].start()
    causal = triangle(True)
    for block in range(2):
        for load in loads[3 * block : 3 * block + 3]:
            load.wait()
        for head in range(heads):
            at = block * heads + head
            row = table_ref[0, at : at + 1, :]
            col = column(row)
            for t in range(BLOCK // TILE):
                later = slice(block * BLOCK + t * TILE, block * BLOCK + (t + 1) * TILE)
                earlier = slice(block * BLOCK, block * BLOCK + (t + 1) * TILE)
                mine = pair(col[t * TILE : (t + 1) * TILE])
                pieces = []
                for s in range(t + 1):
                    gap = mine - row[:, s * TILE : (s + 1) * TILE]
                    if s == t:
                        gap = jnp.where(causal, gap, NEVER)
                    pieces.append(jnp.exp(gap))
                within = pieces[0] if t == 0 else jnp.concatenate(pieces, axis=1)
                scores = nt(query_ref[later, lanes(head)], key_ref[earlier, lanes(head)])
                weights = (scores * within).astype(BF16)
                out_ref[later, lanes(head)] = nn(weights, value_ref[earlier, lanes(head)])


def gate_kernel(gate_hbm, cotangent_hbm, gain_ref, _, out_hbm, gate_ref, cotangent_ref, out_ref, sems):
    loads = []
    for block in range(2):
        at = pl.ds(block * BLOCK, BLOCK)
        for source, target in ((gate_hbm, gate_ref), (cotangent_hbm, cotangent_ref)):
            loads.append(pltpu.make_async_copy(source.at[at], target.at[at], sems.at[len(loads)]))
            loads[-1].start()
    stores = []
    for block in range(2):
        loads[2 * block].wait()
        loads[2 * block + 1].wait()
        tokens = rows_of(block)
        signal = jax.nn.sigmoid(gate_ref[tokens, :].astype(F32))
        out_ref[tokens, :] = cotangent_ref[tokens, :].astype(F32) * gain_ref[...] * signal
        at = pl.ds(block * BLOCK, BLOCK)
        stores.append(pltpu.make_async_copy(out_ref.at[at], out_hbm.at[at], sems.at[len(loads) + block]))
        stores[-1].start()
    for store in stores:
        store.wait()


def attention_kernel(
    heads,
    query_hbm,
    normgrad_hbm,
    first_hbm,
    inner_ref,
    before_ref,
    table_ref,
    out_ref,
    send_ref,
    query_ref,
    normgrad_ref,
    carry_ref,
    first_ref,
    sems,
):
    loads = []
    for block in range(2):
        at = pl.ds(block * BLOCK, BLOCK)
        for source, target in ((query_hbm, query_ref), (normgrad_hbm, normgrad_ref)):
            loads.append(pltpu.make_async_copy(source.at[at], target.at[at], sems.at[len(loads)]))
    loads.insert(2, pltpu.make_async_copy(first_hbm, first_ref, sems.at[4]))
    for load in loads:
        load.start()
    rows = [None] * send_ref.shape[1]
    for block in range(2):
        tokens = rows_of(block)
        for head in range(heads):
            carry_ref[tokens, lanes(head)] = column(
                table_ref[1, block * heads + head : block * heads + head + 1, :]
            )
        for load in ((loads[0],), (loads[2], loads[3]))[block]:
            load.wait()
        for head in range(heads):
            state = before_ref[head]
            if block == 1:
                state = factor_of(table_ref, 0, heads, head) * state + first_ref[head]
            far = halves(nn(query_ref[tokens, lanes(head)], jnp.concatenate(split(state), axis=1)))
            out_ref[tokens, lanes(head)] = (
                inner_ref[tokens, lanes(head)] + carry_ref[tokens, lanes(head)] * far
            )
        loads[(1, 4)[block]].wait()
        for chunk in range(block * BLOCK // CHUNK, (block + 1) * BLOCK // CHUNK):
            at = slice(chunk * CHUNK, (chunk + 1) * CHUNK)
            squares = products = None
            for head in range(heads):
                attention = out_ref[at, lanes(head)]
                square = attention * attention
                product = attention * normgrad_ref[at, lanes(head)]
                squares = square if head == 0 else squares + square
                products = product if head == 0 else products + product
            rows[chunk] = jnp.sum(squares.T, axis=0, keepdims=True)
            rows[len(rows) // 2 + chunk] = jnp.sum(products.T, axis=0, keepdims=True)
    stats = jnp.concatenate(rows, axis=0)
    for target in range(send_ref.shape[0]):
        send_ref[target] = stats


def gradient_kernel(
    heads,
    features,
    got_ref,
    attention_ref,
    normgrad_ref,
    query_ref,
    table_ref,
    carry_ref,
    grad_hbm,
    inverse_ref,
    send_ref,
    attention_hbm,
    second_hbm,
    grad_ref,
    second_ref,
    sems,
):
    stores = [
        pltpu.make_async_copy(attention_ref, attention_hbm, sems.at[0]),
        pltpu.make_async_copy(second_ref, second_hbm, sems.at[1]),
    ]
    stores[0].start()
    stats = got_ref[0]
    for source in range(1, got_ref.shape[0]):
        stats = stats + got_ref[source]
    chunks = stats.shape[0] // 2
    inverses = 1.0 / jnp.sqrt(stats[:chunks] / features + EPS_NORM)
    inners = stats[chunks:] * inverses / features
    inverse_ref[...] = inverses
    for block in (1, 0):
        tokens = rows_of(block)
        for chunk in range(block * BLOCK // CHUNK, (block + 1) * BLOCK // CHUNK):
            at = slice(chunk * CHUNK, (chunk + 1) * CHUNK)
            inverse = column(inverses[chunk : chunk + 1])
            slope = column(inners[chunk : chunk + 1])
            for head in range(heads):
                normed = attention_ref[at, lanes(head)] * inverse
                grad_ref[at, lanes(head)] = (normgrad_ref[at, lanes(head)] - normed * slope) * inverse
        at = pl.ds(block * BLOCK, BLOCK)
        stores.append(pltpu.make_async_copy(grad_ref.at[at], grad_hbm.at[at], sems.at[2 + block]))
        stores[-1].start()
    for block in (1, 0):
        tokens = rows_of(block)
        for head in range(heads):
            weighted = grad_ref[tokens, lanes(head)] * carry_ref[tokens, lanes(head)]
            state = state_of(query_ref[tokens, lanes(head)], weighted)
            if block == 1:
                second_ref[head] = state
            else:
                factor = factor_of(table_ref, 0, heads, head)
                put_slices(
                    send_ref,
                    head,
                    heads,
                    factor * second_ref[head] + state,
                    factor * factor_of(table_ref, 1, heads, head),
                )
        if block == 1:
            stores[1].start()
    for store in stores:
        store.wait()


def back_kernel(heads, block, *refs):
    query_hbm, key_hbm, value_hbm, grad_hbm, first_hbm, before_ref, table_ref, _ = refs[:8]
    if block == 0:
        gquery_hbm, gkey_hbm, gvalue_hbm, gquery_ref, gkey_ref, gvalue_ref = refs[8:14]
        query_ref, key_ref, value_ref, grad_ref, first_ref, sems = refs[14:]
    else:
        gquery_hbm, gkey_ref, gvalue_ref, gquery_ref = refs[9:13]
        query_ref, key_ref, value_ref, grad_ref, first_ref, sems = refs[13:]
    tokens = rows_of(block)
    at = pl.ds(block * BLOCK, BLOCK)
    loads = [
        pltpu.make_async_copy(query_hbm.at[at], query_ref, sems.at[0]),
        pltpu.make_async_copy(key_hbm.at[at], key_ref, sems.at[1]),
        pltpu.make_async_copy(value_hbm.at[at], value_ref, sems.at[2]),
        pltpu.make_async_copy(grad_hbm.at[at], grad_ref, sems.at[3]),
    ]
    if block == 1:
        loads.append(pltpu.make_async_copy(first_hbm, first_ref, sems.at[4]))
    for load in loads:
        load.start()
    causal = triangle(False)
    for load in loads:
        load.wait()
    stores = []
    for head in range(heads):
        state = before_ref[head]
        if block == 1:
            state = factor_of(table_ref, 0, heads, head) * state + first_ref[head]
        place = block * heads + head
        row = table_ref[0, place : place + 1, :]
        col = column(row)
        grad, rest = split(grad_ref[:, lanes(head)])
        high, low = split(state)
        far = halves(nt(grad, jnp.concatenate([high, low], axis=0))) + nt(rest, high)
        gquery = [None] * (BLOCK // TILE)
        for s in range(BLOCK // TILE):
            start = s * TILE
            own = slice(start, start + TILE)
            mine = pair(col[own])
            pieces = []
            for t in range(s, BLOCK // TILE):
                gap = row[:, t * TILE : (t + 1) * TILE] - mine
                if s == t:
                    gap = jnp.where(causal, gap, NEVER)
                pieces.append(jnp.exp(gap))
            within = pieces[0] if len(pieces) == 1 else jnp.concatenate(pieces, axis=1)
            grads = grad[start:]
            key_tile = key_ref[own, lanes(head)]
            queries = query_ref[start:, lanes(head)]
            weights = (nt(key_tile, queries) * within).astype(BF16)
            backs = (nt(value_ref[own, lanes(head)], grads) * within).astype(BF16)
            gkey_ref[own, lanes(head)] = nn(backs, queries)
            gvalue_ref[own, lanes(head)] = nn(weights, grads)
            part = tn(backs, key_tile)
            for t in range(s, BLOCK // TILE):
                piece = part[(t - s) * TILE : (t - s + 1) * TILE]
                gquery[t] = piece if gquery[t] is None else gquery[t] + piece
        total = jnp.concatenate(gquery, axis=0) + column(table_ref[1, place : place + 1, :]) * far
        gquery_ref[:, lanes(head)] = total.astype(BF16)
        lane = pl.ds(head * D_HEAD, D_HEAD)
        moves = [(gquery_ref.at[:, lane], gquery_hbm.at[at, lane])]
        if block == 0:
            moves.append((gkey_ref.at[:, lane], gkey_hbm.at[:, lane]))
            moves.append((gvalue_ref.at[:, lane], gvalue_hbm.at[:, lane]))
        for source, target in moves:
            stores.append(pltpu.make_async_copy(source, target, sems.at[5 + len(stores)]))
            stores[-1].start()
    for store in stores:
        store.wait()


def output_kernel(
    attention_hbm,
    gate_hbm,
    normgrad_hbm,
    inverse_ref,
    gain_ref,
    _,
    attended_hbm,
    ggate_hbm,
    attention_ref,
    gate_ref,
    normgrad_ref,
    attended_ref,
    ggate_ref,
    sems,
):
    loads = []
    for block in range(2):
        at = pl.ds(block * BLOCK, BLOCK)
        for source, target in ((attention_hbm, attention_ref), (gate_hbm, gate_ref), (normgrad_hbm, normgrad_ref)):
            loads.append(pltpu.make_async_copy(source.at[at], target.at[at], sems.at[len(loads)]))
            loads[-1].start()
    stores = []
    for block in range(2):
        for load in loads[3 * block : 3 * block + 3]:
            load.wait()
        for chunk in range(block * BLOCK // CHUNK, (block + 1) * BLOCK // CHUNK):
            tokens = slice(chunk * CHUNK, (chunk + 1) * CHUNK)
            inverse = column(inverse_ref[chunk : chunk + 1, :])
            for head in range(attended_ref.shape[1] // D_HEAD):
                normed = attention_ref[tokens, lanes(head)] * inverse
                signal = jax.nn.sigmoid(gate_ref[tokens, lanes(head)].astype(F32))
                attended_ref[tokens, lanes(head)] = (normed * gain_ref[:, lanes(head)] * signal).astype(BF16)
                ggate_ref[tokens, lanes(head)] = (
                    normgrad_ref[tokens, lanes(head)] * normed * (1.0 - signal)
                ).astype(BF16)
        at = pl.ds(block * BLOCK, BLOCK)
        for source, target in ((attended_ref, attended_hbm), (ggate_ref, ggate_hbm)):
            stores.append(
                pltpu.make_async_copy(source.at[at], target.at[at], sems.at[len(loads) + len(stores)])
            )
            stores[-1].start()
    for store in stores:
        store.wait()


def far_kernel(
    heads,
    key_hbm,
    value_hbm,
    ikey0_hbm,
    ivalue0_hbm,
    second_hbm,
    ikey1_ref,
    ivalue1_ref,
    after_ref,
    table_ref,
    _,
    gkey_hbm,
    gvalue_hbm,
    key_ref,
    value_ref,
    ikey0_ref,
    ivalue0_ref,
    second_ref,
    gkey_ref,
    gvalue_ref,
    sems,
):
    loads = []
    for block in (1, 0):
        at = pl.ds(block * BLOCK, BLOCK)
        moves = [(key_hbm.at[at], key_ref.at[at]), (value_hbm.at[at], value_ref.at[at])]
        if block == 0:
            moves += [(second_hbm, second_ref), (ikey0_hbm, ikey0_ref), (ivalue0_hbm, ivalue0_ref)]
        for source, target in moves:
            loads.append(pltpu.make_async_copy(source, target, sems.at[len(loads)]))
            loads[-1].start()
    stores = []
    for block in (1, 0):
        for load in (loads[2:], loads[:2])[block]:
            load.wait()
        tokens = rows_of(block)
        ikey_ref, ivalue_ref = ((ikey0_ref, ivalue0_ref), (ikey1_ref, ivalue1_ref))[block]
        for head in range(heads):
            state = after_ref[head]
            if block == 0:
                state = factor_of(table_ref, 1, heads, head) * state + second_ref[head]
            high, low = split(state)
            weight = column(table_ref[2, block * heads + head : block * heads + head + 1, :])
            far_key = halves(nt(value_ref[tokens, lanes(head)], jnp.concatenate([high, low], axis=0)))
            far_value = halves(nn(key_ref[tokens, lanes(head)], jnp.concatenate([high, low], axis=1)))
            gkey_ref[tokens, lanes(head)] = (ikey_ref[:, lanes(head)] + weight * far_key).astype(BF16)
            gvalue_ref[tokens, lanes(head)] = (ivalue_ref[:, lanes(head)] + weight * far_value).astype(BF16)
        at = pl.ds(block * BLOCK, BLOCK)
        for source, target in ((gkey_ref, gkey_hbm), (gvalue_ref, gvalue_hbm)):
            stores.append(
                pltpu.make_async_copy(source.at[at], target.at[at], sems.at[len(loads) + len(stores)])
            )
            stores[-1].start()
    for store in stores:
        store.wait()


def sizes():
    return lax.axis_size("ctx"), lax.axis_size("tp")


def exchange(values, axis):
    return lax.all_to_all(values, axis, 0, 0, tiled=True)


def local(query_rows, key_rows, value_rows, gate_logits, norm_gain, log_decay, offsets, cotangent):
    heads = log_decay.shape[0]
    tokens, width = query_rows.shape
    ctx, tp = sizes()
    features = float(tp * width)
    gain = norm_gain.reshape(1, width)
    slice_rows = heads * D_HEAD // ctx
    chunks = tokens // CHUNK
    near, far = (pl.BlockSpec(memory_space=space) for space in (pltpu.VMEM, pltpu.HBM))

    def vmem(dtype, *shape):
        return pltpu.VMEM(shape or (tokens, width), dtype)

    def hbm(dtype, *shape):
        return pltpu.HBM(shape or (tokens, width), dtype)

    full, full_low = vmem(F32), vmem(BF16)
    half, half_low = vmem(F32, BLOCK, width), vmem(BF16, BLOCK, width)
    states = (heads, D_HEAD, D_HEAD)
    sends = vmem(F32, ctx, slice_rows + PAD, D_HEAD)
    slices = vmem(F32, ctx, slice_rows, D_HEAD)
    table = vmem(F32, 4, 2 * heads, BLOCK)

    def call(body, name, in_specs, outs, scratch=(), copies=0, cost=1.0, aliases=None):
        if copies:
            scratch = (*scratch, pltpu.SemaphoreType.DMA((copies,)))
        made = pl.pallas_call(
            body,
            in_specs=in_specs,
            out_specs=[near if out.memory_space == pltpu.VMEM else far for out in outs],
            out_shape=outs,
            scratch_shapes=scratch,
            name=name,
            input_output_aliases=aliases or {},
            cost_estimate=pl.CostEstimate(
                flops=int(cost * 5e8), bytes_accessed=int(cost * 2e6), transcendentals=0
            ),
            compiler_params=pltpu.CompilerParams(vmem_limit_bytes=ROOM),
        )

        def pinned(*arrays):
            return made(
                *(
                    pltpu.with_memory_space_constraint(array, pltpu.VMEM if spec is near else pltpu.HBM)
                    for array, spec in zip(arrays, in_specs)
                )
            )

        return pinned

    tables, send, first = call(
        functools.partial(tables_kernel, heads),
        "tables",
        [far] * 4,
        [table, sends, hbm(F32, *states)],
        scratch=[full_low, full_low, vmem(F32, *states), vmem(F32, heads, tokens), pltpu.SMEM(offsets.shape, jnp.int32)],
        copies=7,
        cost=3,
    )(offsets, log_decay, key_rows, value_rows)

    def scan(backward, got, wait_for, where):
        return call(
            functools.partial(scan_kernel, backward), "scan", [near, where], [slices], cost=0.5
        )(got, wait_for)[0]

    got = exchange(send, "ctx")
    (inner,) = call(
        functools.partial(inner_kernel, heads),
        "inner",
        [far, far, far, near],
        [full],
        scratch=[full_low] * 3,
        copies=6,
        cost=5,
    )(query_rows, key_rows, value_rows, tables)
    prefixes = scan(False, got, inner, near)
    before = exchange(prefixes, "ctx").reshape(states)
    (normgrad,) = call(
        gate_kernel,
        "gate",
        [far, far, near, near],
        [hbm(F32)],
        scratch=[full_low, full_low, full],
        copies=6,
        cost=4,
    )(gate_logits, cotangent, gain, prefixes)

    attention, stats, queries, normgrad_near, carry = call(
        functools.partial(attention_kernel, heads),
        "attention",
        [far, far, far, near, near, near],
        [full, vmem(F32, tp, 2 * chunks, CHUNK), full_low, full, full],
        scratch=[vmem(F32, *states)],
        copies=5,
        cost=2,
    )(query_rows, normgrad, first, inner, before, tables)
    stats = exchange(stats, "tp")

    grad, inverse, send, attention_far, second = call(
        functools.partial(gradient_kernel, heads, features),
        "gradient",
        [near] * 6,
        [hbm(F32), vmem(F32, chunks, CHUNK), sends, hbm(F32), hbm(F32, *states)],
        scratch=[full, vmem(F32, *states)],
        copies=4,
        cost=3,
    )(stats, attention, normgrad_near, queries, tables, carry)
    got = exchange(send, "ctx")

    loaded = [half_low, half_low, half_low, half, vmem(F32, *states)]
    back_specs = [far] * 5 + [near] * 3
    grad_query, ikey0, ivalue0 = call(
        functools.partial(back_kernel, heads, 0),
        "back0",
        back_specs,
        [hbm(BF16), hbm(F32, BLOCK, width), hbm(F32, BLOCK, width)],
        scratch=[half_low, half, half, *loaded],
        copies=5 + 3 * heads,
        cost=5,
    )(query_rows, key_rows, value_rows, grad, first, before, tables, send)
    suffixes = scan(True, got, grad_query, far)
    after = exchange(suffixes, "ctx").reshape(states)
    grad_query, ikey1, ivalue1 = call(
        functools.partial(back_kernel, heads, 1),
        "back1",
        [*back_specs, far],
        [hbm(BF16), half, half],
        scratch=[half_low, *loaded],
        copies=5 + heads,
        cost=5,
        aliases={8: 0},
    )(query_rows, key_rows, value_rows, grad, first, before, tables, suffixes, grad_query)
    attended, grad_gate = call(
        output_kernel,
        "output",
        [far, far, far, near, near, near],
        [hbm(BF16)] * 2,
        scratch=[full, full_low, full, full_low, full_low],
        copies=10,
        cost=3,
    )(attention_far, gate_logits, normgrad, inverse, gain, suffixes)
    grad_key, grad_value = call(
        functools.partial(far_kernel, heads),
        "far",
        [far] * 5 + [near] * 4 + [far],
        [hbm(BF16)] * 2,
        scratch=[full_low, full_low, half, half, vmem(F32, *states), full_low, full_low],
        copies=11,
        cost=3,
    )(key_rows, value_rows, ikey0, ivalue0, second, ikey1, ivalue1, after, tables, attended)
    return (attended, grad_query, grad_key, grad_value, grad_gate)


def solution(mesh):
    placed = (
        P("ctx", "tp"),
        P("ctx", "tp"),
        P("ctx", "tp"),
        P("ctx", "tp"),
        P("tp"),
        P("tp", "ctx"),
        P(),
        P("ctx", "tp"),
    )
    return jax.shard_map(
        local,
        mesh=mesh,
        in_specs=placed,
        out_specs=(P("ctx", "tp"), P("ctx", "tp"), P("ctx", "tp"), P("ctx", "tp"), P("ctx", "tp")),
        check_vma=False,
    )
```

```python
import functools

import jax
import jax.numpy as jnp
from jax import lax
from jax.experimental import pallas as pl
from jax.experimental.pallas import tpu as pltpu
from jax.sharding import PartitionSpec as P

D_HEAD = 128
BLOCK = 512
TILE = 256
CHUNK = 128
EPS_NORM = 1e-06
RESET = -128.0
NEVER = -1e30
F32 = jnp.float32
BF16 = jnp.bfloat16
PAD = 8
ROOM = 24 << 20


def nn(a, b):
    return lax.dot_general(a, b, (((1,), (0,)), ((), ())), preferred_element_type=F32)


def nt(a, b):
    return lax.dot_general(a, b, (((1,), (1,)), ((), ())), preferred_element_type=F32)


def tn(a, b):
    return lax.dot_general(a, b, (((0,), (0,)), ((), ())), preferred_element_type=F32)


def split(x):
    high = x.astype(BF16)
    return high, (x - high.astype(F32)).astype(BF16)


def halves(x):
    return x[:, :D_HEAD] + x[:, D_HEAD:]


def column(row):
    return jnp.broadcast_to(row, (CHUNK, row.shape[1])).T


def triangle(rows_are_later):
    first = lax.broadcasted_iota(jnp.int32, (TILE, TILE), 0)
    second = lax.broadcasted_iota(jnp.int32, (TILE, TILE), 1)
    return first >= second if rows_are_later else first <= second


def state_of(rows, weighted):
    high, low = split(weighted)
    return halves(tn(rows, jnp.concatenate([high, low], axis=1)))


def lanes(head):
    return slice(head * D_HEAD, (head + 1) * D_HEAD)


def rows_of(block):
    return slice(block * BLOCK, (block + 1) * BLOCK)


def pair(tile):
    return jnp.concatenate([tile, tile], axis=1)


def put_slices(send_ref, head, heads, total, factor):
    parts = send_ref.shape[0] // heads
    rows = send_ref.shape[1] - PAD
    both = jnp.broadcast_to(factor, (PAD, D_HEAD))
    for part in range(parts):
        send_ref[head * parts + part, :rows, :] = total[part * rows : (part + 1) * rows]
        send_ref[head * parts + part, rows:, :] = both


def factor_of(table_ref, block, heads, head):
    at = block * heads + head
    return table_ref[3, at : at + 1, :D_HEAD]


def tables_kernel(
    heads,
    offsets_hbm,
    decay_hbm,
    key_hbm,
    value_hbm,
    table_ref,
    send_ref,
    first_hbm,
    key_ref,
    value_ref,
    first_ref,
    decay_ref,
    offsets_ref,
    sems,
):
    loads = [
        pltpu.make_async_copy(offsets_hbm, offsets_ref, sems.at[0]),
        pltpu.make_async_copy(decay_hbm, decay_ref, sems.at[1]),
    ]
    for block in range(2):
        at = pl.ds(block * BLOCK, BLOCK)
        for source, target in ((key_hbm, key_ref), (value_hbm, value_ref)):
            loads.append(pltpu.make_async_copy(source.at[at], target.at[at], sems.at[len(loads)]))
    for load in loads:
        load.start()
    loads[0].wait()
    loads[1].wait()
    decay = decay_ref[...]
    running = jnp.concatenate([decay[:, :BLOCK], decay[:, BLOCK:]], axis=0)
    lane = lax.broadcasted_iota(jnp.int32, running.shape, 1)
    row = lax.broadcasted_iota(jnp.int32, running.shape, 0)
    position = lax.axis_index("ctx") * decay.shape[1] + (row // heads) * BLOCK + lane
    starts = position == offsets_ref[0]
    for index in range(1, offsets_ref.shape[0]):
        starts = starts | (position == offsets_ref[index])
    running = jnp.where(starts, running + RESET, running)
    step = 1
    while step < BLOCK:
        running = running + jnp.where(lane >= step, pltpu.roll(running, step, axis=1), 0.0)
        step *= 2
    last = jnp.broadcast_to(running[:, BLOCK - 1 :], running.shape)
    until_last = jnp.exp(jnp.minimum(last - running, 0.0))
    table_ref[0] = running
    table_ref[1] = jnp.exp(running)
    table_ref[2] = until_last
    table_ref[3] = jnp.exp(last)
    for block in range(2):
        loads[2 + 2 * block].wait()
        loads[3 + 2 * block].wait()
        tokens = rows_of(block)
        for head in range(heads):
            at = block * heads + head
            weighted = value_ref[tokens, lanes(head)].astype(F32) * column(until_last[at : at + 1])
            state = state_of(key_ref[tokens, lanes(head)], weighted)
            if block == 0:
                first_ref[head] = state
            else:
                factor = factor_of(table_ref, 1, heads, head)
                put_slices(
                    send_ref,
                    head,
                    heads,
                    factor * first_ref[head] + state,
                    factor * factor_of(table_ref, 0, heads, head),
                )
        if block == 0:
            store = pltpu.make_async_copy(first_ref, first_hbm, sems.at[len(loads)])
            store.start()
    store.wait()


def scan_kernel(backward, got_ref, _, out_ref):
    count, rows, _ = out_ref.shape
    carried = jnp.zeros(out_ref.shape[1:], F32)
    for step in range(count):
        source = count - 1 - step if backward else step
        out_ref[source] = carried
        carried = got_ref[source, rows : rows + 1, :] * carried + got_ref[source, :rows, :]


def inner_kernel(heads, query_hbm, key_hbm, value_hbm, table_ref, out_ref, query_ref, key_ref, value_ref, sems):
    loads = []
    for block in range(2):
        at = pl.ds(block * BLOCK, BLOCK)
        for source, target in ((query_hbm, query_ref), (key_hbm, key_ref), (value_hbm, value_ref)):
            loads.append(pltpu.make_async_copy(source.at[at], target.at[at], sems.at[len(loads)]))
            loads[-1].start()
    causal = triangle(True)
    for block in range(2):
        for load in loads[3 * block : 3 * block + 3]:
            load.wait()
        for head in range(heads):
            at = block * heads + head
            row = table_ref[0, at : at + 1, :]
            col = column(row)
            for t in range(BLOCK // TILE):
                later = slice(block * BLOCK + t * TILE, block * BLOCK + (t + 1) * TILE)
                earlier = slice(block * BLOCK, block * BLOCK + (t + 1) * TILE)
                mine = pair(col[t * TILE : (t + 1) * TILE])
                pieces = []
                for s in range(t + 1):
                    gap = mine - row[:, s * TILE : (s + 1) * TILE]
                    if s == t:
                        gap = jnp.where(causal, gap, NEVER)
                    pieces.append(jnp.exp(gap))
                within = pieces[0] if t == 0 else jnp.concatenate(pieces, axis=1)
                scores = nt(query_ref[later, lanes(head)], key_ref[earlier, lanes(head)])
                weights = (scores * within).astype(BF16)
                out_ref[later, lanes(head)] = nn(weights, value_ref[earlier, lanes(head)])


def gate_kernel(gate_hbm, cotangent_hbm, gain_ref, _, out_hbm, gate_ref, cotangent_ref, out_ref, sems):
    loads = []
    for block in range(2):
        at = pl.ds(block * BLOCK, BLOCK)
        for source, target in ((gate_hbm, gate_ref), (cotangent_hbm, cotangent_ref)):
            loads.append(pltpu.make_async_copy(source.at[at], target.at[at], sems.at[len(loads)]))
            loads[-1].start()
    stores = []
    for block in range(2):
        loads[2 * block].wait()
        loads[2 * block + 1].wait()
        tokens = rows_of(block)
        signal = jax.nn.sigmoid(gate_ref[tokens, :].astype(F32))
        out_ref[tokens, :] = cotangent_ref[tokens, :].astype(F32) * gain_ref[...] * signal
        at = pl.ds(block * BLOCK, BLOCK)
        stores.append(pltpu.make_async_copy(out_ref.at[at], out_hbm.at[at], sems.at[len(loads) + block]))
        stores[-1].start()
    for store in stores:
        store.wait()


def attention_kernel(
    heads,
    query_hbm,
    normgrad_hbm,
    first_hbm,
    inner_ref,
    before_ref,
    table_ref,
    out_ref,
    send_ref,
    query_ref,
    normgrad_ref,
    carry_ref,
    first_ref,
    sems,
):
    loads = []
    for block in range(2):
        at = pl.ds(block * BLOCK, BLOCK)
        for source, target in ((query_hbm, query_ref), (normgrad_hbm, normgrad_ref)):
            loads.append(pltpu.make_async_copy(source.at[at], target.at[at], sems.at[len(loads)]))
    loads.insert(2, pltpu.make_async_copy(first_hbm, first_ref, sems.at[4]))
    for load in loads:
        load.start()
    rows = [None] * send_ref.shape[1]
    for block in range(2):
        tokens = rows_of(block)
        for head in range(heads):
            carry_ref[tokens, lanes(head)] = column(
                table_ref[1, block * heads + head : block * heads + head + 1, :]
            )
        for load in ((loads[0],), (loads[2], loads[3]))[block]:
            load.wait()
        for head in range(heads):
            state = before_ref[head]
            if block == 1:
                state = factor_of(table_ref, 0, heads, head) * state + first_ref[head]
            far = halves(nn(query_ref[tokens, lanes(head)], jnp.concatenate(split(state), axis=1)))
            out_ref[tokens, lanes(head)] = (
                inner_ref[tokens, lanes(head)] + carry_ref[tokens, lanes(head)] * far
            )
        loads[(1, 4)[block]].wait()
        for chunk in range(block * BLOCK // CHUNK, (block + 1) * BLOCK // CHUNK):
            at = slice(chunk * CHUNK, (chunk + 1) * CHUNK)
            squares = products = None
            for head in range(heads):
                attention = out_ref[at, lanes(head)]
                square = attention * attention
                product = attention * normgrad_ref[at, lanes(head)]
                squares = square if head == 0 else squares + square
                products = product if head == 0 else products + product
            rows[chunk] = jnp.sum(squares.T, axis=0, keepdims=True)
            rows[len(rows) // 2 + chunk] = jnp.sum(products.T, axis=0, keepdims=True)
    stats = jnp.concatenate(rows, axis=0)
    for target in range(send_ref.shape[0]):
        send_ref[target] = stats


def gradient_kernel(
    heads,
    features,
    gate_hbm,
    got_ref,
    attention_ref,
    normgrad_ref,
    query_ref,
    table_ref,
    carry_ref,
    gain_ref,
    first_high_ref,
    second_high_ref,
    rest_hbm,
    send_ref,
    second_hbm,
    attended_hbm,
    ggate_hbm,
    rest_ref,
    gate_ref,
    grad_ref,
    second_ref,
    attended_ref,
    ggate_ref,
    normed_ref,
    sems,
):
    load = pltpu.make_async_copy(gate_hbm, gate_ref, sems.at[0])
    load.start()
    stores = []

    def store(source, target):
        stores.append(pltpu.make_async_copy(source, target, sems.at[1 + len(stores)]))
        stores[-1].start()

    stats = got_ref[0]
    for source in range(1, got_ref.shape[0]):
        stats = stats + got_ref[source]
    chunks = stats.shape[0] // 2
    inverses = 1.0 / jnp.sqrt(stats[:chunks] / features + EPS_NORM)
    inners = stats[chunks:] * inverses / features
    for chunk in range(chunks):
        at = slice(chunk * CHUNK, (chunk + 1) * CHUNK)
        inverse = column(inverses[chunk : chunk + 1])
        slope = column(inners[chunk : chunk + 1])
        for head in range(heads):
            normed = attention_ref[at, lanes(head)] * inverse
            grad = (normgrad_ref[at, lanes(head)] - normed * slope) * inverse
            normed_ref[at, lanes(head)] = normed
            high, rest = split(grad)
            within = slice(chunk * CHUNK % BLOCK, chunk * CHUNK % BLOCK + CHUNK)
            high_ref = first_high_ref if at.stop <= BLOCK else second_high_ref
            high_ref[within, lanes(head)] = high
            rest_ref[at, lanes(head)] = rest
            grad_ref[at, lanes(head)] = grad * carry_ref[at, lanes(head)]
    store(rest_ref, rest_hbm)
    load.wait()
    for block in (1, 0):
        for chunk in range(block * BLOCK // CHUNK, (block + 1) * BLOCK // CHUNK):
            at = slice(chunk * CHUNK, (chunk + 1) * CHUNK)
            for head in range(heads):
                normed = normed_ref[at, lanes(head)]
                signal = jax.nn.sigmoid(gate_ref[at, lanes(head)].astype(F32))
                attended_ref[at, lanes(head)] = (normed * gain_ref[:, lanes(head)] * signal).astype(BF16)
                ggate_ref[at, lanes(head)] = (
                    normgrad_ref[at, lanes(head)] * normed * (1.0 - signal)
                ).astype(BF16)
        rows = pl.ds(block * BLOCK, BLOCK)
        store(attended_ref.at[rows], attended_hbm.at[rows])
        store(ggate_ref.at[rows], ggate_hbm.at[rows])
    for block in (1, 0):
        tokens = rows_of(block)
        for head in range(heads):
            state = state_of(query_ref[tokens, lanes(head)], grad_ref[tokens, lanes(head)])
            if block == 1:
                second_ref[head] = state
            else:
                factor = factor_of(table_ref, 0, heads, head)
                put_slices(
                    send_ref,
                    head,
                    heads,
                    factor * second_ref[head] + state,
                    factor * factor_of(table_ref, 1, heads, head),
                )
        if block == 1:
            store(second_ref, second_hbm)
    for move in stores:
        move.wait()


def back_kernel(heads, block, *refs):
    query_hbm, key_hbm, value_hbm, rest_hbm, first_hbm, high_ref, before_ref, table_ref = refs[:8]
    gquery_hbm, gkey_ref, gvalue_ref = refs[-10:-7]
    gquery_ref, query_ref, key_ref, value_ref, rest_ref, first_ref, sems = refs[-7:]
    at = pl.ds(block * BLOCK, BLOCK)
    loads = [
        pltpu.make_async_copy(key_hbm.at[at], key_ref, sems.at[0]),
        pltpu.make_async_copy(query_hbm.at[at], query_ref, sems.at[1]),
        pltpu.make_async_copy(value_hbm.at[at], value_ref, sems.at[2]),
        pltpu.make_async_copy(rest_hbm.at[at], rest_ref, sems.at[3]),
    ]
    if block == 1:
        loads.append(pltpu.make_async_copy(first_hbm, first_ref, sems.at[4]))
    for load in loads:
        load.start()
    for load in loads:
        load.wait()
    causal = triangle(False)
    tiles = range(BLOCK // TILE)
    for head in range(heads):
        state = before_ref[head]
        if block == 1:
            state = factor_of(table_ref, 0, heads, head) * state + first_ref[head]
        place = block * heads + head
        row = table_ref[0, place : place + 1, :]
        col = column(row)
        grad = high_ref[:, lanes(head)]
        high, low = split(state)
        states = jnp.concatenate([pair(high), jnp.concatenate([low, jnp.zeros_like(low)], axis=1)], axis=0)
        far = halves(nt(jnp.concatenate([grad, rest_ref[:, lanes(head)]], axis=1), states))
        gkey = [None for _ in tiles]
        gvalue = [None for _ in tiles]
        for t in tiles:
            later = slice(t * TILE, (t + 1) * TILE)
            earlier = slice(0, (t + 1) * TILE)
            pieces = []
            for s in range(t + 1):
                gap = row[:, later] - pair(col[s * TILE : (s + 1) * TILE])
                if s == t:
                    gap = jnp.where(causal, gap, NEVER)
                pieces.append(jnp.exp(gap))
            within = pieces[0] if t == 0 else jnp.concatenate(pieces, axis=0)
            keys = key_ref[earlier, lanes(head)]
            queries = query_ref[later, lanes(head)]
            grads = grad[later]
            weights = (nt(keys, queries) * within).astype(BF16)
            backs = (nt(value_ref[earlier, lanes(head)], grads) * within).astype(BF16)
            for sums, part in ((gkey, nn(backs, queries)), (gvalue, nn(weights, grads))):
                for s in range(t + 1):
                    piece = part[s * TILE : (s + 1) * TILE]
                    sums[s] = piece if sums[s] is None else sums[s] + piece
            carry = column(table_ref[1, place : place + 1, later])
            gquery_ref[later, lanes(head)] = (tn(backs, keys) + carry * far[later]).astype(BF16)
        for s in tiles:
            own = slice(s * TILE, (s + 1) * TILE)
            gkey_ref[own, lanes(head)] = gkey[s].astype(BF16)
            gvalue_ref[own, lanes(head)] = gvalue[s].astype(BF16)
    store = pltpu.make_async_copy(gquery_ref, gquery_hbm.at[at], sems.at[5])
    store.start()
    store.wait()


def far_kernel(
    heads,
    key_hbm,
    value_hbm,
    second_hbm,
    ikey0_ref,
    ivalue0_ref,
    ikey1_ref,
    ivalue1_ref,
    after_ref,
    table_ref,
    _,
    gkey_hbm,
    gvalue_hbm,
    key_ref,
    value_ref,
    second_ref,
    gkey_ref,
    gvalue_ref,
    sems,
):
    loads = []
    for block in (1, 0):
        at = pl.ds(block * BLOCK, BLOCK)
        moves = [(key_hbm.at[at], key_ref.at[at]), (value_hbm.at[at], value_ref.at[at])]
        if block == 0:
            moves.insert(0, (second_hbm, second_ref))
        for source, target in moves:
            loads.append(pltpu.make_async_copy(source, target, sems.at[len(loads)]))
            loads[-1].start()
    stores = []
    for block in (1, 0):
        for load in (loads[2:], loads[:2])[block]:
            load.wait()
        tokens = rows_of(block)
        ikey_ref, ivalue_ref = ((ikey0_ref, ivalue0_ref), (ikey1_ref, ivalue1_ref))[block]
        for head in range(heads):
            state = after_ref[head]
            if block == 0:
                state = factor_of(table_ref, 1, heads, head) * state + second_ref[head]
            high, low = split(state)
            weight = column(table_ref[2, block * heads + head : block * heads + head + 1, :])
            far_key = halves(nt(value_ref[tokens, lanes(head)], jnp.concatenate([high, low], axis=0)))
            far_value = halves(nn(key_ref[tokens, lanes(head)], jnp.concatenate([high, low], axis=1)))
            gkey_ref[tokens, lanes(head)] = (ikey_ref[:, lanes(head)].astype(F32) + weight * far_key).astype(BF16)
            gvalue_ref[tokens, lanes(head)] = (
                ivalue_ref[:, lanes(head)].astype(F32) + weight * far_value
            ).astype(BF16)
        at = pl.ds(block * BLOCK, BLOCK)
        for source, target in ((gkey_ref, gkey_hbm), (gvalue_ref, gvalue_hbm)):
            stores.append(
                pltpu.make_async_copy(source.at[at], target.at[at], sems.at[len(loads) + len(stores)])
            )
            stores[-1].start()
    for store in stores:
        store.wait()


def sizes():
    return lax.axis_size("ctx"), lax.axis_size("tp")


def exchange(values, axis):
    return lax.all_to_all(values, axis, 0, 0, tiled=True)


def local(query_rows, key_rows, value_rows, gate_logits, norm_gain, log_decay, offsets, cotangent):
    heads = log_decay.shape[0]
    tokens, width = query_rows.shape
    ctx, tp = sizes()
    features = float(tp * width)
    gain = norm_gain.reshape(1, width)
    slice_rows = heads * D_HEAD // ctx
    chunks = tokens // CHUNK
    near, far = (pl.BlockSpec(memory_space=space) for space in (pltpu.VMEM, pltpu.HBM))

    def vmem(dtype, *shape):
        return pltpu.VMEM(shape or (tokens, width), dtype)

    def hbm(dtype, *shape):
        return pltpu.HBM(shape or (tokens, width), dtype)

    full, full_low = vmem(F32), vmem(BF16)
    half, half_low = vmem(F32, BLOCK, width), vmem(BF16, BLOCK, width)
    states = (heads, D_HEAD, D_HEAD)
    sends = vmem(F32, ctx, slice_rows + PAD, D_HEAD)
    slices = vmem(F32, ctx, slice_rows, D_HEAD)
    table = vmem(F32, 4, 2 * heads, BLOCK)

    def call(body, name, in_specs, outs, scratch=(), copies=0, cost=1.0, aliases=None):
        if copies:
            scratch = (*scratch, pltpu.SemaphoreType.DMA((copies,)))
        made = pl.pallas_call(
            body,
            in_specs=in_specs,
            out_specs=[near if out.memory_space == pltpu.VMEM else far for out in outs],
            out_shape=outs,
            scratch_shapes=scratch,
            name=name,
            input_output_aliases=aliases or {},
            cost_estimate=pl.CostEstimate(
                flops=int(cost * 5e8), bytes_accessed=int(cost * 2e6), transcendentals=0
            ),
            compiler_params=pltpu.CompilerParams(vmem_limit_bytes=ROOM),
        )

        def pinned(*arrays):
            return made(
                *(
                    pltpu.with_memory_space_constraint(array, pltpu.VMEM if spec is near else pltpu.HBM)
                    for array, spec in zip(arrays, in_specs)
                )
            )

        return pinned

    tables, send, first = call(
        functools.partial(tables_kernel, heads),
        "tables",
        [far] * 4,
        [table, sends, hbm(F32, *states)],
        scratch=[full_low, full_low, vmem(F32, *states), vmem(F32, heads, tokens), pltpu.SMEM(offsets.shape, jnp.int32)],
        copies=7,
        cost=3,
    )(offsets, log_decay, key_rows, value_rows)

    def scan(backward, got, wait_for, where):
        return call(
            functools.partial(scan_kernel, backward), "scan", [near, where], [slices], cost=0.5
        )(got, wait_for)[0]

    got = exchange(send, "ctx")
    (inner,) = call(
        functools.partial(inner_kernel, heads),
        "inner",
        [far, far, far, near],
        [full],
        scratch=[full_low] * 3,
        copies=6,
        cost=5,
    )(query_rows, key_rows, value_rows, tables)
    prefixes = scan(False, got, inner, near)
    before = exchange(prefixes, "ctx").reshape(states)
    (normgrad,) = call(
        gate_kernel,
        "gate",
        [far, far, near, near],
        [hbm(F32)],
        scratch=[full_low, full_low, full],
        copies=6,
        cost=4,
    )(gate_logits, cotangent, gain, prefixes)

    attention, stats, queries, normgrad_near, carry = call(
        functools.partial(attention_kernel, heads),
        "attention",
        [far, far, far, near, near, near],
        [full, vmem(F32, tp, 2 * chunks, CHUNK), full_low, full, full],
        scratch=[vmem(F32, *states)],
        copies=5,
        cost=2,
    )(query_rows, normgrad, first, inner, before, tables)
    stats = exchange(stats, "tp")

    first_grad, second_grad, rest, send, second, attended, grad_gate = call(
        functools.partial(gradient_kernel, heads, features),
        "gradient",
        [far] + [near] * 7,
        [half_low, half_low, hbm(BF16), sends, hbm(F32, *states), hbm(BF16), hbm(BF16)],
        scratch=[full_low, full_low, full, vmem(F32, *states), full_low, full_low, full],
        copies=7,
        cost=3,
    )(gate_logits, stats, attention, normgrad_near, queries, tables, carry, gain)
    got = exchange(send, "ctx")

    loaded = [half_low] * 5 + [vmem(F32, *states)]
    back_specs = [far] * 5 + [near] * 3
    sources = (query_rows, key_rows, value_rows, rest, first)
    outs = [hbm(BF16), half_low, half_low]
    grad_query, ikey0, ivalue0 = call(
        functools.partial(back_kernel, heads, 0), "back0", back_specs, outs, scratch=loaded, copies=6, cost=5
    )(*sources, first_grad, before, tables)
    suffixes = scan(True, got, grad_query, far)
    after = exchange(suffixes, "ctx").reshape(states)
    grad_query, ikey1, ivalue1 = call(
        functools.partial(back_kernel, heads, 1),
        "back1",
        [*back_specs, near, far],
        outs,
        scratch=loaded,
        copies=6,
        cost=5,
        aliases={9: 0},
    )(*sources, second_grad, before, tables, suffixes, grad_query)
    grad_key, grad_value = call(
        functools.partial(far_kernel, heads),
        "far",
        [far] * 3 + [near] * 6 + [far],
        [hbm(BF16)] * 2,
        scratch=[full_low, full_low, vmem(F32, *states), full_low, full_low],
        copies=9,
        cost=3,
    )(key_rows, value_rows, second, ikey0, ivalue0, ikey1, ivalue1, after, tables, grad_query)
    return (attended, grad_query, grad_key, grad_value, grad_gate)


def solution(mesh):
    placed = (
        P("ctx", "tp"),
        P("ctx", "tp"),
        P("ctx", "tp"),
        P("ctx", "tp"),
        P("tp"),
        P("tp", "ctx"),
        P(),
        P("ctx", "tp"),
    )
    return jax.shard_map(
        local,
        mesh=mesh,
        in_specs=placed,
        out_specs=(P("ctx", "tp"), P("ctx", "tp"), P("ctx", "tp"), P("ctx", "tp"), P("ctx", "tp")),
        check_vma=False,
    )
```

```python
import functools

import jax
import jax.numpy as jnp
from jax import lax
from jax.experimental import pallas as pl
from jax.experimental.pallas import tpu as pltpu
from jax.sharding import PartitionSpec as P

D_HEAD = 128
BLOCK = 512
TILE = 256
CHUNK = 128
EPS_NORM = 1e-06
RESET = -128.0
NEVER = -1e30
F32 = jnp.float32
BF16 = jnp.bfloat16
PAD = 8
ROOM = 24 << 20


def nn(a, b):
    return lax.dot_general(a, b, (((1,), (0,)), ((), ())), preferred_element_type=F32)


def nt(a, b):
    return lax.dot_general(a, b, (((1,), (1,)), ((), ())), preferred_element_type=F32)


def tn(a, b):
    return lax.dot_general(a, b, (((0,), (0,)), ((), ())), preferred_element_type=F32)


def split(x):
    high = x.astype(BF16)
    return high, (x - high.astype(F32)).astype(BF16)


def halves(x):
    return x[:, :D_HEAD] + x[:, D_HEAD:]


def column(row):
    return jnp.broadcast_to(row, (CHUNK, row.shape[1])).T


def triangle(rows_are_later):
    first = lax.broadcasted_iota(jnp.int32, (TILE, TILE), 0)
    second = lax.broadcasted_iota(jnp.int32, (TILE, TILE), 1)
    return first >= second if rows_are_later else first <= second


def state_of(rows, weighted):
    high, low = split(weighted)
    return halves(tn(rows, jnp.concatenate([high, low], axis=1)))


def lanes(head):
    return slice(head * D_HEAD, (head + 1) * D_HEAD)


def rows_of(block):
    return slice(block * BLOCK, (block + 1) * BLOCK)


def pair(tile):
    return jnp.concatenate([tile, tile], axis=1)


def put_slices(send_ref, head, heads, total, factor):
    parts = send_ref.shape[0] // heads
    rows = send_ref.shape[1] - PAD
    both = jnp.broadcast_to(factor, (PAD, D_HEAD))
    for part in range(parts):
        send_ref[head * parts + part, :rows, :] = total[part * rows : (part + 1) * rows]
        send_ref[head * parts + part, rows:, :] = both


def factor_of(table_ref, block, heads, head):
    at = block * heads + head
    return table_ref[3, at : at + 1, :D_HEAD]


def tables_kernel(
    heads,
    offsets_hbm,
    decay_hbm,
    key_hbm,
    value_hbm,
    table_ref,
    send_ref,
    first_hbm,
    key_ref,
    value_ref,
    first_ref,
    decay_ref,
    offsets_ref,
    sems,
):
    loads = [
        pltpu.make_async_copy(offsets_hbm, offsets_ref, sems.at[0]),
        pltpu.make_async_copy(decay_hbm, decay_ref, sems.at[1]),
    ]
    for block in range(2):
        at = pl.ds(block * BLOCK, BLOCK)
        for source, target in ((key_hbm, key_ref), (value_hbm, value_ref)):
            loads.append(pltpu.make_async_copy(source.at[at], target.at[at], sems.at[len(loads)]))
    for load in loads:
        load.start()
    loads[0].wait()
    loads[1].wait()
    decay = decay_ref[...]
    running = jnp.concatenate([decay[:, :BLOCK], decay[:, BLOCK:]], axis=0)
    lane = lax.broadcasted_iota(jnp.int32, running.shape, 1)
    row = lax.broadcasted_iota(jnp.int32, running.shape, 0)
    position = lax.axis_index("ctx") * decay.shape[1] + (row // heads) * BLOCK + lane
    starts = position == offsets_ref[0]
    for index in range(1, offsets_ref.shape[0]):
        starts = starts | (position == offsets_ref[index])
    running = jnp.where(starts, running + RESET, running)
    step = 1
    while step < BLOCK:
        running = running + jnp.where(lane >= step, pltpu.roll(running, step, axis=1), 0.0)
        step *= 2
    last = jnp.broadcast_to(running[:, BLOCK - 1 :], running.shape)
    until_last = jnp.exp(jnp.minimum(last - running, 0.0))
    table_ref[0] = running
    table_ref[1] = jnp.exp(running)
    table_ref[2] = until_last
    table_ref[3] = jnp.exp(last)
    for block in range(2):
        loads[2 + 2 * block].wait()
        loads[3 + 2 * block].wait()
        tokens = rows_of(block)
        for head in range(heads):
            at = block * heads + head
            weighted = value_ref[tokens, lanes(head)].astype(F32) * column(until_last[at : at + 1])
            state = state_of(key_ref[tokens, lanes(head)], weighted)
            if block == 0:
                first_ref[head] = state
            else:
                factor = factor_of(table_ref, 1, heads, head)
                put_slices(
                    send_ref,
                    head,
                    heads,
                    factor * first_ref[head] + state,
                    factor * factor_of(table_ref, 0, heads, head),
                )
        if block == 0:
            store = pltpu.make_async_copy(first_ref, first_hbm, sems.at[len(loads)])
            store.start()
    store.wait()


def scan_kernel(backward, got_ref, _, out_ref):
    count, rows, _ = out_ref.shape
    carried = jnp.zeros(out_ref.shape[1:], F32)
    for step in range(count):
        source = count - 1 - step if backward else step
        out_ref[source] = carried
        carried = got_ref[source, rows : rows + 1, :] * carried + got_ref[source, :rows, :]


def inner_kernel(heads, query_hbm, key_hbm, value_hbm, table_ref, out_ref, query_ref, key_ref, value_ref, sems):
    loads = []
    for block in range(2):
        at = pl.ds(block * BLOCK, BLOCK)
        for source, target in ((query_hbm, query_ref), (key_hbm, key_ref), (value_hbm, value_ref)):
            loads.append(pltpu.make_async_copy(source.at[at], target.at[at], sems.at[len(loads)]))
            loads[-1].start()
    causal = triangle(True)
    for block in range(2):
        for load in loads[3 * block : 3 * block + 3]:
            load.wait()
        for head in range(heads):
            at = block * heads + head
            row = table_ref[0, at : at + 1, :]
            col = column(row)
            for t in range(BLOCK // TILE):
                later = slice(block * BLOCK + t * TILE, block * BLOCK + (t + 1) * TILE)
                earlier = slice(block * BLOCK, block * BLOCK + (t + 1) * TILE)
                mine = pair(col[t * TILE : (t + 1) * TILE])
                pieces = []
                for s in range(t + 1):
                    gap = mine - row[:, s * TILE : (s + 1) * TILE]
                    if s == t:
                        gap = jnp.where(causal, gap, NEVER)
                    pieces.append(jnp.exp(gap))
                within = pieces[0] if t == 0 else jnp.concatenate(pieces, axis=1)
                scores = nt(query_ref[later, lanes(head)], key_ref[earlier, lanes(head)])
                weights = (scores * within).astype(BF16)
                out_ref[later, lanes(head)] = nn(weights, value_ref[earlier, lanes(head)])


def gate_kernel(gate_hbm, cotangent_hbm, gain_ref, _, out_hbm, gate_ref, cotangent_ref, out_ref, sems):
    loads = []
    for block in range(2):
        at = pl.ds(block * BLOCK, BLOCK)
        for source, target in ((gate_hbm, gate_ref), (cotangent_hbm, cotangent_ref)):
            loads.append(pltpu.make_async_copy(source.at[at], target.at[at], sems.at[len(loads)]))
            loads[-1].start()
    stores = []
    for block in range(2):
        loads[2 * block].wait()
        loads[2 * block + 1].wait()
        tokens = rows_of(block)
        signal = jax.nn.sigmoid(gate_ref[tokens, :].astype(F32))
        out_ref[tokens, :] = cotangent_ref[tokens, :].astype(F32) * gain_ref[...] * signal
        at = pl.ds(block * BLOCK, BLOCK)
        stores.append(pltpu.make_async_copy(out_ref.at[at], out_hbm.at[at], sems.at[len(loads) + block]))
        stores[-1].start()
    for store in stores:
        store.wait()


def attention_kernel(
    heads,
    query_hbm,
    normgrad_hbm,
    first_hbm,
    gate_hbm,
    inner_ref,
    before_ref,
    table_ref,
    out_ref,
    send_ref,
    query_ref,
    normgrad_ref,
    carry_ref,
    gate_ref,
    first_ref,
    sems,
):
    loads = []
    for block in range(2):
        at = pl.ds(block * BLOCK, BLOCK)
        for source, target in ((query_hbm, query_ref), (normgrad_hbm, normgrad_ref)):
            loads.append(pltpu.make_async_copy(source.at[at], target.at[at], sems.at[len(loads)]))
    loads.insert(2, pltpu.make_async_copy(first_hbm, first_ref, sems.at[4]))
    last = pltpu.make_async_copy(gate_hbm, gate_ref, sems.at[5])
    for load in (*loads, last):
        load.start()
    rows = [None] * send_ref.shape[1]
    for block in range(2):
        tokens = rows_of(block)
        for head in range(heads):
            carry_ref[tokens, lanes(head)] = column(
                table_ref[1, block * heads + head : block * heads + head + 1, :]
            )
        for load in ((loads[0], loads[1]), (loads[2], loads[3], loads[4]))[block]:
            load.wait()
        for head in range(heads):
            state = before_ref[head]
            if block == 1:
                state = factor_of(table_ref, 0, heads, head) * state + first_ref[head]
            far = halves(nn(query_ref[tokens, lanes(head)], jnp.concatenate(split(state), axis=1)))
            out_ref[tokens, lanes(head)] = (
                inner_ref[tokens, lanes(head)] + carry_ref[tokens, lanes(head)] * far
            )
        for chunk in range(block * BLOCK // CHUNK, (block + 1) * BLOCK // CHUNK):
            at = slice(chunk * CHUNK, (chunk + 1) * CHUNK)
            squares = products = None
            for head in range(heads):
                attention = out_ref[at, lanes(head)]
                square = attention * attention
                product = attention * normgrad_ref[at, lanes(head)]
                squares = square if head == 0 else squares + square
                products = product if head == 0 else products + product
            rows[chunk] = jnp.sum(squares.T, axis=0, keepdims=True)
            rows[len(rows) // 2 + chunk] = jnp.sum(products.T, axis=0, keepdims=True)
    stats = jnp.concatenate(rows, axis=0)
    for target in range(send_ref.shape[0]):
        send_ref[target] = stats
    last.wait()


def gradient_kernel(
    heads,
    features,
    gate_ref,
    got_ref,
    attention_ref,
    normgrad_ref,
    query_ref,
    table_ref,
    carry_ref,
    gain_ref,
    first_high_ref,
    second_high_ref,
    rest_hbm,
    send_ref,
    second_hbm,
    attended_hbm,
    ggate_hbm,
    rest_ref,
    grad_ref,
    second_ref,
    attended_ref,
    ggate_ref,
    normed_ref,
    sems,
):
    stores = []

    def store(source, target):
        stores.append(pltpu.make_async_copy(source, target, sems.at[len(stores)]))
        stores[-1].start()

    stats = got_ref[0]
    for source in range(1, got_ref.shape[0]):
        stats = stats + got_ref[source]
    chunks = stats.shape[0] // 2
    inverses = 1.0 / jnp.sqrt(stats[:chunks] / features + EPS_NORM)
    inners = stats[chunks:] * inverses / features
    for chunk in range(chunks):
        at = slice(chunk * CHUNK, (chunk + 1) * CHUNK)
        inverse = column(inverses[chunk : chunk + 1])
        slope = column(inners[chunk : chunk + 1])
        for head in range(heads):
            normed = attention_ref[at, lanes(head)] * inverse
            grad = (normgrad_ref[at, lanes(head)] - normed * slope) * inverse
            normed_ref[at, lanes(head)] = normed
            high, rest = split(grad)
            within = slice(chunk * CHUNK % BLOCK, chunk * CHUNK % BLOCK + CHUNK)
            high_ref = first_high_ref if at.stop <= BLOCK else second_high_ref
            high_ref[within, lanes(head)] = high
            rest_ref[at, lanes(head)] = rest
            grad_ref[at, lanes(head)] = grad * carry_ref[at, lanes(head)]
    store(rest_ref, rest_hbm)
    for block in (1, 0):
        for chunk in range(block * BLOCK // CHUNK, (block + 1) * BLOCK // CHUNK):
            at = slice(chunk * CHUNK, (chunk + 1) * CHUNK)
            for head in range(heads):
                normed = normed_ref[at, lanes(head)]
                signal = jax.nn.sigmoid(gate_ref[at, lanes(head)].astype(F32))
                attended_ref[at, lanes(head)] = (normed * gain_ref[:, lanes(head)] * signal).astype(BF16)
                ggate_ref[at, lanes(head)] = (
                    normgrad_ref[at, lanes(head)] * normed * (1.0 - signal)
                ).astype(BF16)
        rows = pl.ds(block * BLOCK, BLOCK)
        store(attended_ref.at[rows], attended_hbm.at[rows])
        store(ggate_ref.at[rows], ggate_hbm.at[rows])
    for block in (1, 0):
        tokens = rows_of(block)
        for head in range(heads):
            state = state_of(query_ref[tokens, lanes(head)], grad_ref[tokens, lanes(head)])
            if block == 1:
                second_ref[head] = state
            else:
                factor = factor_of(table_ref, 0, heads, head)
                put_slices(
                    send_ref,
                    head,
                    heads,
                    factor * second_ref[head] + state,
                    factor * factor_of(table_ref, 1, heads, head),
                )
        if block == 1:
            store(second_ref, second_hbm)
    for move in stores:
        move.wait()


def back_kernel(heads, block, *refs):
    query_hbm, key_hbm, value_hbm, rest_hbm, first_hbm, high_ref, before_ref, table_ref = refs[:8]
    if block == 0:
        gquery_hbm, gkey_hbm, gvalue_hbm, gkey_ref, gvalue_ref, key_ref, value_ref = refs[-11:-4]
    else:
        gquery_hbm, gkey_ref, gvalue_ref, key_ref, value_ref, first_ref = refs[-10:-4]
    gquery_ref, query_ref, rest_ref, sems = refs[-4:]
    at = pl.ds(block * BLOCK, BLOCK)
    loads = [
        pltpu.make_async_copy(key_hbm.at[at], key_ref, sems.at[0]),
        pltpu.make_async_copy(query_hbm.at[at], query_ref, sems.at[1]),
        pltpu.make_async_copy(value_hbm.at[at], value_ref, sems.at[2]),
        pltpu.make_async_copy(rest_hbm.at[at], rest_ref, sems.at[3]),
    ]
    if block == 1:
        loads.append(pltpu.make_async_copy(first_hbm, first_ref, sems.at[4]))
    for load in loads:
        load.start()
    for load in loads:
        load.wait()
    causal = triangle(False)
    tiles = range(BLOCK // TILE)
    for head in range(heads):
        place = block * heads + head
        row = table_ref[0, place : place + 1, :]
        col = column(row)
        grad = high_ref[:, lanes(head)]
        gquery = []
        state = before_ref[head]
        if block == 1:
            state = factor_of(table_ref, 0, heads, head) * state + first_ref[head]
        high, low = split(state)
        states = jnp.concatenate([pair(high), jnp.concatenate([low, jnp.zeros_like(low)], axis=1)], axis=0)
        far = halves(nt(jnp.concatenate([grad, rest_ref[:, lanes(head)]], axis=1), states))
        gkey = [None for _ in tiles]
        gvalue = [None for _ in tiles]
        for t in tiles:
            later = slice(t * TILE, (t + 1) * TILE)
            earlier = slice(0, (t + 1) * TILE)
            pieces = []
            for s in range(t + 1):
                gap = row[:, later] - pair(col[s * TILE : (s + 1) * TILE])
                if s == t:
                    gap = jnp.where(causal, gap, NEVER)
                pieces.append(jnp.exp(gap))
            within = pieces[0] if t == 0 else jnp.concatenate(pieces, axis=0)
            keys = key_ref[earlier, lanes(head)]
            queries = query_ref[later, lanes(head)]
            grads = grad[later]
            weights = (nt(keys, queries) * within).astype(BF16)
            backs = (nt(value_ref[earlier, lanes(head)], grads) * within).astype(BF16)
            for sums, part in ((gkey, nn(backs, queries)), (gvalue, nn(weights, grads))):
                for s in range(t + 1):
                    piece = part[s * TILE : (s + 1) * TILE]
                    sums[s] = piece if sums[s] is None else sums[s] + piece
            gquery.append(tn(backs, keys))
        total = jnp.concatenate(gquery, axis=0) + column(table_ref[1, place : place + 1, :]) * far
        gquery_ref[:, lanes(head)] = total.astype(BF16)
        for s in tiles:
            own = slice(s * TILE, (s + 1) * TILE)
            gkey_ref[own, lanes(head)] = gkey[s].astype(BF16)
            gvalue_ref[own, lanes(head)] = gvalue[s].astype(BF16)
    moves = [(gquery_ref, gquery_hbm.at[at])]
    if block == 0:
        moves += [(gkey_ref, gkey_hbm), (gvalue_ref, gvalue_hbm)]
    stores = [
        pltpu.make_async_copy(source, target, sems.at[len(loads) + index])
        for index, (source, target) in enumerate(moves)
    ]
    for store in stores:
        store.start()
    for store in stores:
        store.wait()


def far_kernel(
    heads,
    key_hbm,
    value_hbm,
    ikey_hbm,
    ivalue_hbm,
    second_hbm,
    ikey1_ref,
    ivalue1_ref,
    key1_ref,
    value1_ref,
    after_ref,
    table_ref,
    _,
    gkey_hbm,
    gvalue_hbm,
    key0_ref,
    value0_ref,
    ikey0_ref,
    ivalue0_ref,
    second_ref,
    gkey_ref,
    gvalue_ref,
    sems,
):
    at = pl.ds(0, BLOCK)
    loads = [
        pltpu.make_async_copy(source, target, sems.at[index])
        for index, (source, target) in enumerate(
            (
                (second_hbm, second_ref),
                (value_hbm.at[at], value0_ref),
                (key_hbm.at[at], key0_ref),
                (ikey_hbm, ikey0_ref),
                (ivalue_hbm, ivalue0_ref),
            )
        )
    ]
    for load in loads:
        load.start()
    stores = []
    for block in (1, 0):
        if block == 0:
            for load in loads:
                load.wait()
        key_ref, value_ref, ikey_ref, ivalue_ref = (
            (key0_ref, value0_ref, ikey0_ref, ivalue0_ref),
            (key1_ref, value1_ref, ikey1_ref, ivalue1_ref),
        )[block]
        pieces = (slice(0, BLOCK),) if block == 1 else (slice(0, TILE), slice(TILE, BLOCK))
        for piece in pieces:
            out = slice(block * BLOCK + piece.start, block * BLOCK + piece.stop)
            for head in range(heads):
                state = after_ref[head]
                if block == 0:
                    state = factor_of(table_ref, 1, heads, head) * state + second_ref[head]
                high, low = split(state)
                place = block * heads + head
                weight = column(table_ref[2, place : place + 1, piece])
                far_key = halves(nt(value_ref[piece, lanes(head)], jnp.concatenate([high, low], axis=0)))
                far_value = halves(nn(key_ref[piece, lanes(head)], jnp.concatenate([high, low], axis=1)))
                gkey_ref[out, lanes(head)] = (
                    ikey_ref[piece, lanes(head)].astype(F32) + weight * far_key
                ).astype(BF16)
                gvalue_ref[out, lanes(head)] = (
                    ivalue_ref[piece, lanes(head)].astype(F32) + weight * far_value
                ).astype(BF16)
            at = pl.ds(out.start, out.stop - out.start)
            for source, target in ((gkey_ref, gkey_hbm), (gvalue_ref, gvalue_hbm)):
                stores.append(
                    pltpu.make_async_copy(source.at[at], target.at[at], sems.at[len(loads) + len(stores)])
                )
                stores[-1].start()
    for store in stores:
        store.wait()


def sizes():
    return lax.axis_size("ctx"), lax.axis_size("tp")


def exchange(values, axis):
    return lax.all_to_all(values, axis, 0, 0, tiled=True)


def local(query_rows, key_rows, value_rows, gate_logits, norm_gain, log_decay, offsets, cotangent):
    heads = log_decay.shape[0]
    tokens, width = query_rows.shape
    ctx, tp = sizes()
    features = float(tp * width)
    gain = norm_gain.reshape(1, width)
    slice_rows = heads * D_HEAD // ctx
    chunks = tokens // CHUNK
    near, far = (pl.BlockSpec(memory_space=space) for space in (pltpu.VMEM, pltpu.HBM))

    def vmem(dtype, *shape):
        return pltpu.VMEM(shape or (tokens, width), dtype)

    def hbm(dtype, *shape):
        return pltpu.HBM(shape or (tokens, width), dtype)

    full, full_low = vmem(F32), vmem(BF16)
    half, half_low = vmem(F32, BLOCK, width), vmem(BF16, BLOCK, width)
    states = (heads, D_HEAD, D_HEAD)
    sends = vmem(F32, ctx, slice_rows + PAD, D_HEAD)
    slices = vmem(F32, ctx, slice_rows, D_HEAD)
    table = vmem(F32, 4, 2 * heads, BLOCK)

    def call(body, name, in_specs, outs, scratch=(), copies=0, cost=1.0, aliases=None):
        if copies:
            scratch = (*scratch, pltpu.SemaphoreType.DMA((copies,)))
        made = pl.pallas_call(
            body,
            in_specs=in_specs,
            out_specs=[near if out.memory_space == pltpu.VMEM else far for out in outs],
            out_shape=outs,
            scratch_shapes=scratch,
            name=name,
            input_output_aliases=aliases or {},
            cost_estimate=pl.CostEstimate(
                flops=int(cost * 5e8), bytes_accessed=int(cost * 2e6), transcendentals=0
            ),
            compiler_params=pltpu.CompilerParams(vmem_limit_bytes=ROOM),
        )

        def pinned(*arrays):
            return made(
                *(
                    pltpu.with_memory_space_constraint(array, pltpu.VMEM if spec is near else pltpu.HBM)
                    for array, spec in zip(arrays, in_specs)
                )
            )

        return pinned

    tables, send, first = call(
        functools.partial(tables_kernel, heads),
        "tables",
        [far] * 4,
        [table, sends, hbm(F32, *states)],
        scratch=[full_low, full_low, vmem(F32, *states), vmem(F32, heads, tokens), pltpu.SMEM(offsets.shape, jnp.int32)],
        copies=7,
        cost=3,
    )(offsets, log_decay, key_rows, value_rows)

    def scan(backward, got, wait_for, where):
        return call(
            functools.partial(scan_kernel, backward), "scan", [near, where], [slices], cost=0.5
        )(got, wait_for)[0]

    got = exchange(send, "ctx")
    (inner,) = call(
        functools.partial(inner_kernel, heads),
        "inner",
        [far, far, far, near],
        [full],
        scratch=[full_low] * 3,
        copies=6,
        cost=5,
    )(query_rows, key_rows, value_rows, tables)
    prefixes = scan(False, got, inner, near)
    before = exchange(prefixes, "ctx").reshape(states)
    (normgrad,) = call(
        gate_kernel,
        "gate",
        [far, far, near, near],
        [hbm(F32)],
        scratch=[full_low, full_low, full],
        copies=6,
        cost=4,
    )(gate_logits, cotangent, gain, prefixes)

    attention, stats, queries, normgrad_near, carry, gates = call(
        functools.partial(attention_kernel, heads),
        "attention",
        [far, far, far, far, near, near, near],
        [full, vmem(F32, tp, 2 * chunks, CHUNK), full_low, full, full, full_low],
        scratch=[vmem(F32, *states)],
        copies=6,
        cost=2,
    )(query_rows, normgrad, first, gate_logits, inner, before, tables)
    stats = exchange(stats, "tp")

    first_grad, second_grad, rest, send, second, attended, grad_gate = call(
        functools.partial(gradient_kernel, heads, features),
        "gradient",
        [near] * 8,
        [half_low, half_low, hbm(BF16), sends, hbm(F32, *states), hbm(BF16), hbm(BF16)],
        scratch=[full_low, full, vmem(F32, *states), full_low, full_low, full],
        copies=6,
        cost=3,
    )(gates, stats, attention, normgrad_near, queries, tables, carry, gain)
    got = exchange(send, "ctx")

    back_specs = [far] * 5 + [near] * 3
    sources = (query_rows, key_rows, value_rows, rest, first)
    half_hbm = hbm(BF16, BLOCK, width)
    grad_query, ikey0, ivalue0 = call(
        functools.partial(back_kernel, heads, 0),
        "back0",
        back_specs,
        [hbm(BF16), half_hbm, half_hbm],
        scratch=[half_low] * 7,
        copies=7,
        cost=5,
    )(*sources, first_grad, before, tables)
    suffixes = scan(True, got, grad_query, far)
    after = exchange(suffixes, "ctx").reshape(states)
    grad_query, ikey1, ivalue1, keys1, values1 = call(
        functools.partial(back_kernel, heads, 1),
        "back1",
        [*back_specs, near, far],
        [hbm(BF16), half_low, half_low, half_low, half_low],
        scratch=[vmem(F32, *states), half_low, half_low, half_low],
        copies=6,
        cost=5,
        aliases={9: 0},
    )(*sources, second_grad, before, tables, suffixes, grad_query)
    grad_key, grad_value = call(
        functools.partial(far_kernel, heads),
        "far",
        [far] * 5 + [near] * 6 + [far],
        [hbm(BF16)] * 2,
        scratch=[half_low] * 4 + [vmem(F32, *states), full_low, full_low],
        copies=11,
        cost=3,
    )(key_rows, value_rows, ikey0, ivalue0, second, ikey1, ivalue1, keys1, values1, after, tables, grad_query)
    return (attended, grad_query, grad_key, grad_value, grad_gate)


def solution(mesh):
    placed = (
        P("ctx", "tp"),
        P("ctx", "tp"),
        P("ctx", "tp"),
        P("ctx", "tp"),
        P("tp"),
        P("tp", "ctx"),
        P(),
        P("ctx", "tp"),
    )
    return jax.shard_map(
        local,
        mesh=mesh,
        in_specs=placed,
        out_specs=(P("ctx", "tp"), P("ctx", "tp"), P("ctx", "tp"), P("ctx", "tp"), P("ctx", "tp")),
        check_vma=False,
    )
```

```python
import functools

import jax
import jax.numpy as jnp
from jax import lax
from jax.experimental import pallas as pl
from jax.experimental.pallas import tpu as pltpu
from jax.sharding import PartitionSpec as P

D_HEAD = 128
BLOCK = 512
TILE = 256
CHUNK = 128
EPS_NORM = 1e-06
RESET = -128.0
NEVER = -1e30
F32 = jnp.float32
BF16 = jnp.bfloat16
PAD = 8
ROOM = 24 << 20


def nn(a, b):
    return lax.dot_general(a, b, (((1,), (0,)), ((), ())), preferred_element_type=F32)


def nt(a, b):
    return lax.dot_general(a, b, (((1,), (1,)), ((), ())), preferred_element_type=F32)


def tn(a, b):
    return lax.dot_general(a, b, (((0,), (0,)), ((), ())), preferred_element_type=F32)


def split(x):
    high = x.astype(BF16)
    return high, (x - high.astype(F32)).astype(BF16)


def halves(x):
    return x[:, :D_HEAD] + x[:, D_HEAD:]


def column(row):
    return jnp.broadcast_to(row, (CHUNK, row.shape[1])).T


def triangle(rows_are_later):
    first = lax.broadcasted_iota(jnp.int32, (TILE, TILE), 0)
    second = lax.broadcasted_iota(jnp.int32, (TILE, TILE), 1)
    return first >= second if rows_are_later else first <= second


def state_of(rows, weighted):
    high, low = split(weighted)
    return halves(tn(rows, jnp.concatenate([high, low], axis=1)))


def lanes(head):
    return slice(head * D_HEAD, (head + 1) * D_HEAD)


def rows_of(block):
    return slice(block * BLOCK, (block + 1) * BLOCK)


def pair(tile):
    return jnp.concatenate([tile, tile], axis=1)


def decays(row, col, t, causal):
    pieces = []
    for s in range(t + 1):
        gap = row[:, t * TILE : (t + 1) * TILE] - pair(col[s * TILE : (s + 1) * TILE])
        if s == t:
            gap = jnp.where(causal, gap, NEVER)
        pieces.append(jnp.exp(gap))
    return pieces[0] if t == 0 else jnp.concatenate(pieces, axis=0)


def put_slices(send_ref, head, heads, total, factor):
    parts = send_ref.shape[0] // heads
    rows = send_ref.shape[1] - PAD
    both = jnp.broadcast_to(factor, (PAD, D_HEAD))
    for part in range(parts):
        send_ref[head * parts + part, :rows, :] = total[part * rows : (part + 1) * rows]
        send_ref[head * parts + part, rows:, :] = both


def factor_of(table_ref, block, heads, head):
    at = block * heads + head
    return table_ref[3, at : at + 1, :D_HEAD]


def tables_kernel(
    heads,
    offsets_hbm,
    decay_hbm,
    key_hbm,
    value_hbm,
    table_ref,
    send_ref,
    first_hbm,
    key_ref,
    value_ref,
    first_ref,
    decay_ref,
    offsets_ref,
    sems,
):
    loads = [
        pltpu.make_async_copy(offsets_hbm, offsets_ref, sems.at[0]),
        pltpu.make_async_copy(decay_hbm, decay_ref, sems.at[1]),
    ]
    for block in range(2):
        at = pl.ds(block * BLOCK, BLOCK)
        for source, target in ((key_hbm, key_ref), (value_hbm, value_ref)):
            loads.append(pltpu.make_async_copy(source.at[at], target.at[at], sems.at[len(loads)]))
    for load in loads:
        load.start()
    loads[0].wait()
    loads[1].wait()
    decay = decay_ref[...]
    running = jnp.concatenate([decay[:, :BLOCK], decay[:, BLOCK:]], axis=0)
    lane = lax.broadcasted_iota(jnp.int32, running.shape, 1)
    row = lax.broadcasted_iota(jnp.int32, running.shape, 0)
    position = lax.axis_index("ctx") * decay.shape[1] + (row // heads) * BLOCK + lane
    starts = position == offsets_ref[0]
    for index in range(1, offsets_ref.shape[0]):
        starts = starts | (position == offsets_ref[index])
    running = jnp.where(starts, running + RESET, running)
    step = 1
    while step < BLOCK:
        running = running + jnp.where(lane >= step, pltpu.roll(running, step, axis=1), 0.0)
        step *= 2
    last = jnp.broadcast_to(running[:, BLOCK - 1 :], running.shape)
    until_last = jnp.exp(jnp.minimum(last - running, 0.0))
    table_ref[0] = running
    table_ref[1] = jnp.exp(running)
    table_ref[2] = until_last
    table_ref[3] = jnp.exp(last)
    for block in range(2):
        loads[2 + 2 * block].wait()
        loads[3 + 2 * block].wait()
        tokens = rows_of(block)
        for head in range(heads):
            at = block * heads + head
            weighted = value_ref[tokens, lanes(head)].astype(F32) * column(until_last[at : at + 1])
            state = state_of(key_ref[tokens, lanes(head)], weighted)
            if block == 0:
                first_ref[head] = state
            else:
                factor = factor_of(table_ref, 1, heads, head)
                put_slices(
                    send_ref,
                    head,
                    heads,
                    factor * first_ref[head] + state,
                    factor * factor_of(table_ref, 0, heads, head),
                )
        if block == 0:
            store = pltpu.make_async_copy(first_ref, first_hbm, sems.at[len(loads)])
            store.start()
    store.wait()


def scan_kernel(backward, got_ref, _, out_ref):
    count, rows, _ = out_ref.shape
    carried = jnp.zeros(out_ref.shape[1:], F32)
    for step in range(count):
        source = count - 1 - step if backward else step
        out_ref[source] = carried
        carried = got_ref[source, rows : rows + 1, :] * carried + got_ref[source, :rows, :]


def inner_kernel(
    heads,
    query_hbm,
    key_hbm,
    value_hbm,
    table_ref,
    out_ref,
    early_hbm,
    late_hbm,
    query_ref,
    key_ref,
    value_ref,
    early_ref,
    late_ref,
    sems,
):
    loads = []
    for block in (1, 0):
        at = pl.ds(block * BLOCK, BLOCK)
        for source, target in ((query_hbm, query_ref), (key_hbm, key_ref), (value_hbm, value_ref)):
            loads.append(pltpu.make_async_copy(source.at[at], target.at[at], sems.at[len(loads)]))
            loads[-1].start()
    causal = triangle(False)
    stores = [
        pltpu.make_async_copy(early_ref, early_hbm, sems.at[6]),
        pltpu.make_async_copy(late_ref, late_hbm, sems.at[7]),
    ]
    for block in (1, 0):
        for load in loads[3 - 3 * block : 6 - 3 * block]:
            load.wait()
        for head in range(heads):
            place = block * heads + head
            row = table_ref[0, place : place + 1, :]
            col = column(row)
            for t, weights_ref in enumerate((early_ref, late_ref)):
                later = slice(block * BLOCK + t * TILE, block * BLOCK + (t + 1) * TILE)
                earlier = slice(block * BLOCK, block * BLOCK + (t + 1) * TILE)
                within = decays(row, col, t, causal)
                scores = nt(key_ref[earlier, lanes(head)], query_ref[later, lanes(head)])
                weights = (scores * within).astype(BF16)
                if block == 1:
                    weights_ref[head] = weights
                out_ref[later, lanes(head)] = tn(weights, value_ref[earlier, lanes(head)])
        if block == 1:
            for store in stores:
                store.start()
    for store in stores:
        store.wait()


def gate_kernel(gate_hbm, cotangent_hbm, gain_ref, _, out_hbm, gate_ref, cotangent_ref, out_ref, sems):
    loads = []
    for block in range(2):
        at = pl.ds(block * BLOCK, BLOCK)
        for source, target in ((gate_hbm, gate_ref), (cotangent_hbm, cotangent_ref)):
            loads.append(pltpu.make_async_copy(source.at[at], target.at[at], sems.at[len(loads)]))
            loads[-1].start()
    stores = []
    for block in range(2):
        loads[2 * block].wait()
        loads[2 * block + 1].wait()
        tokens = rows_of(block)
        signal = jax.nn.sigmoid(gate_ref[tokens, :].astype(F32))
        out_ref[tokens, :] = cotangent_ref[tokens, :].astype(F32) * gain_ref[...] * signal
        at = pl.ds(block * BLOCK, BLOCK)
        stores.append(pltpu.make_async_copy(out_ref.at[at], out_hbm.at[at], sems.at[len(loads) + block]))
        stores[-1].start()
    for store in stores:
        store.wait()


def attention_kernel(
    heads,
    query_hbm,
    normgrad_hbm,
    first_hbm,
    gate_hbm,
    inner_ref,
    before_ref,
    table_ref,
    out_ref,
    send_ref,
    query_ref,
    normgrad_ref,
    carry_ref,
    gate_ref,
    first_ref,
    sems,
):
    loads = []
    for block in range(2):
        at = pl.ds(block * BLOCK, BLOCK)
        for source, target in ((query_hbm, query_ref), (normgrad_hbm, normgrad_ref)):
            loads.append(pltpu.make_async_copy(source.at[at], target.at[at], sems.at[len(loads)]))
    loads.insert(2, pltpu.make_async_copy(first_hbm, first_ref, sems.at[4]))
    last = pltpu.make_async_copy(gate_hbm, gate_ref, sems.at[5])
    for load in (*loads, last):
        load.start()
    rows = [None] * send_ref.shape[1]
    for block in range(2):
        tokens = rows_of(block)
        for head in range(heads):
            carry_ref[tokens, lanes(head)] = column(
                table_ref[1, block * heads + head : block * heads + head + 1, :]
            )
        for load in ((loads[0], loads[1]), (loads[2], loads[3], loads[4]))[block]:
            load.wait()
        for head in range(heads):
            state = before_ref[head]
            if block == 1:
                state = factor_of(table_ref, 0, heads, head) * state + first_ref[head]
            far = halves(nn(query_ref[tokens, lanes(head)], jnp.concatenate(split(state), axis=1)))
            out_ref[tokens, lanes(head)] = (
                inner_ref[tokens, lanes(head)] + carry_ref[tokens, lanes(head)] * far
            )
        for chunk in range(block * BLOCK // CHUNK, (block + 1) * BLOCK // CHUNK):
            at = slice(chunk * CHUNK, (chunk + 1) * CHUNK)
            squares = products = None
            for head in range(heads):
                attention = out_ref[at, lanes(head)]
                square = attention * attention
                product = attention * normgrad_ref[at, lanes(head)]
                squares = square if head == 0 else squares + square
                products = product if head == 0 else products + product
            rows[chunk] = jnp.sum(squares.T, axis=0, keepdims=True)
            rows[len(rows) // 2 + chunk] = jnp.sum(products.T, axis=0, keepdims=True)
    stats = jnp.concatenate(rows, axis=0)
    for target in range(send_ref.shape[0]):
        send_ref[target] = stats
    last.wait()


def gradient_kernel(
    heads,
    features,
    gate_ref,
    got_ref,
    attention_ref,
    normgrad_ref,
    query_ref,
    table_ref,
    carry_ref,
    gain_ref,
    first_high_ref,
    second_high_ref,
    rest_hbm,
    send_ref,
    second_hbm,
    attended_hbm,
    ggate_hbm,
    rest_ref,
    grad_ref,
    second_ref,
    attended_ref,
    ggate_ref,
    normed_ref,
    sems,
):
    stores = []

    def store(source, target):
        stores.append(pltpu.make_async_copy(source, target, sems.at[len(stores)]))
        stores[-1].start()

    stats = got_ref[0]
    for source in range(1, got_ref.shape[0]):
        stats = stats + got_ref[source]
    chunks = stats.shape[0] // 2
    inverses = 1.0 / jnp.sqrt(stats[:chunks] / features + EPS_NORM)
    inners = stats[chunks:] * inverses / features
    for chunk in range(chunks):
        at = slice(chunk * CHUNK, (chunk + 1) * CHUNK)
        inverse = column(inverses[chunk : chunk + 1])
        slope = column(inners[chunk : chunk + 1])
        for head in range(heads):
            normed = attention_ref[at, lanes(head)] * inverse
            grad = (normgrad_ref[at, lanes(head)] - normed * slope) * inverse
            normed_ref[at, lanes(head)] = normed
            high, rest = split(grad)
            within = slice(chunk * CHUNK % BLOCK, chunk * CHUNK % BLOCK + CHUNK)
            high_ref = first_high_ref if at.stop <= BLOCK else second_high_ref
            high_ref[within, lanes(head)] = high
            rest_ref[at, lanes(head)] = rest
            grad_ref[at, lanes(head)] = grad * carry_ref[at, lanes(head)]
    store(rest_ref, rest_hbm)
    for block in (1, 0):
        for chunk in range(block * BLOCK // CHUNK, (block + 1) * BLOCK // CHUNK):
            at = slice(chunk * CHUNK, (chunk + 1) * CHUNK)
            for head in range(heads):
                normed = normed_ref[at, lanes(head)]
                signal = jax.nn.sigmoid(gate_ref[at, lanes(head)].astype(F32))
                attended_ref[at, lanes(head)] = (normed * gain_ref[:, lanes(head)] * signal).astype(BF16)
                ggate_ref[at, lanes(head)] = (
                    normgrad_ref[at, lanes(head)] * normed * (1.0 - signal)
                ).astype(BF16)
        rows = pl.ds(block * BLOCK, BLOCK)
        store(attended_ref.at[rows], attended_hbm.at[rows])
        store(ggate_ref.at[rows], ggate_hbm.at[rows])
    for block in (1, 0):
        tokens = rows_of(block)
        for head in range(heads):
            state = state_of(query_ref[tokens, lanes(head)], grad_ref[tokens, lanes(head)])
            if block == 1:
                second_ref[head] = state
            else:
                factor = factor_of(table_ref, 0, heads, head)
                put_slices(
                    send_ref,
                    head,
                    heads,
                    factor * second_ref[head] + state,
                    factor * factor_of(table_ref, 1, heads, head),
                )
        if block == 1:
            store(second_ref, second_hbm)
    for move in stores:
        move.wait()


def back_kernel(heads, block, *refs):
    query_hbm, key_hbm, value_hbm, rest_hbm, high_ref, before_ref, table_ref = refs[:7]
    gquery_ref, query_ref, rest_ref, sems = refs[-4:]
    at = pl.ds(block * BLOCK, BLOCK)
    if block == 0:
        gquery_hbm, gkey_hbm, gvalue_hbm, gkey_ref, gvalue_ref, key_ref, value_ref = refs[-11:-4]
    else:
        first_hbm, early_hbm, late_hbm = refs[7:10]
        gquery_hbm, gkey_ref, gvalue_ref, key_ref, value_ref, first_ref, early_ref, late_ref = refs[-12:-4]
    moves = [
        (value_hbm.at[at], value_ref),
        (key_hbm.at[at], key_ref),
        (query_hbm.at[at], query_ref),
        (rest_hbm.at[at], rest_ref),
    ]
    if block == 1:
        moves += [(first_hbm, first_ref), (early_hbm, early_ref), (late_hbm, late_ref)]
    loads = [
        pltpu.make_async_copy(source, target, sems.at[index]) for index, (source, target) in enumerate(moves)
    ]
    now = 5 if block == 1 else 4
    for load in loads:
        load.start()
    for load in loads[:now]:
        load.wait()
    causal = triangle(False)
    tiles = range(BLOCK // TILE)
    for head in range(heads):
        place = block * heads + head
        row = table_ref[0, place : place + 1, :]
        col = column(row)
        grad = high_ref[:, lanes(head)]
        state = before_ref[head]
        if block == 1:
            state = factor_of(table_ref, 0, heads, head) * state + first_ref[head]
        high, low = split(state)
        states = jnp.concatenate([pair(high), jnp.concatenate([low, jnp.zeros_like(low)], axis=1)], axis=0)
        far = halves(nt(jnp.concatenate([grad, rest_ref[:, lanes(head)]], axis=1), states))
        gquery = []
        gkey = []
        gvalue = []
        for t in tiles:
            later = slice(t * TILE, (t + 1) * TILE)
            earlier = slice(0, (t + 1) * TILE)
            within = decays(row, col, t, causal)
            keys = key_ref[earlier, lanes(head)]
            queries = query_ref[later, lanes(head)]
            if block == 0:
                weights = (nt(keys, queries) * within).astype(BF16)
            backs = (nt(value_ref[earlier, lanes(head)], grad[later]) * within).astype(BF16)
            gkey.append(nn(backs, queries))
            if block == 0:
                gvalue.append(nn(weights, grad[later]))
            gquery.append(tn(backs, keys))
        total = jnp.concatenate(gquery, axis=0) + column(table_ref[1, place : place + 1, :]) * far
        gquery_ref[:, lanes(head)] = total.astype(BF16)
        gkey_ref[:TILE, lanes(head)] = (gkey[0] + gkey[1][:TILE]).astype(BF16)
        gkey_ref[TILE:, lanes(head)] = gkey[1][TILE:].astype(BF16)
        if block == 0:
            gvalue_ref[:TILE, lanes(head)] = (gvalue[0] + gvalue[1][:TILE]).astype(BF16)
            gvalue_ref[TILE:, lanes(head)] = gvalue[1][TILE:].astype(BF16)
    for load in loads[now:]:
        load.wait()
    for head in range(heads if block == 1 else 0):
        grad = high_ref[:, lanes(head)]
        early = nn(early_ref[head], grad[:TILE])
        late = nn(late_ref[head], grad[TILE:])
        gvalue_ref[:TILE, lanes(head)] = (early + late[:TILE]).astype(BF16)
        gvalue_ref[TILE:, lanes(head)] = late[TILE:].astype(BF16)
    moves = [(gquery_ref, gquery_hbm.at[at])]
    if block == 0:
        moves += [(gkey_ref, gkey_hbm), (gvalue_ref, gvalue_hbm)]
    stores = [
        pltpu.make_async_copy(source, target, sems.at[len(loads) + index])
        for index, (source, target) in enumerate(moves)
    ]
    for store in stores:
        store.start()
    for store in stores:
        store.wait()


def far_kernel(
    heads,
    key_hbm,
    value_hbm,
    ikey_hbm,
    ivalue_hbm,
    second_hbm,
    ikey1_ref,
    ivalue1_ref,
    key1_ref,
    value1_ref,
    after_ref,
    table_ref,
    _,
    gkey_hbm,
    gvalue_hbm,
    key0_ref,
    value0_ref,
    ikey0_ref,
    ivalue0_ref,
    second_ref,
    gkey_ref,
    gvalue_ref,
    sems,
):
    at = pl.ds(0, BLOCK)
    loads = [
        pltpu.make_async_copy(source, target, sems.at[index])
        for index, (source, target) in enumerate(
            (
                (second_hbm, second_ref),
                (value_hbm.at[at], value0_ref),
                (key_hbm.at[at], key0_ref),
                (ikey_hbm, ikey0_ref),
                (ivalue_hbm, ivalue0_ref),
            )
        )
    ]
    for load in loads:
        load.start()
    stores = []
    for block in (1, 0):
        if block == 0:
            for load in loads:
                load.wait()
        key_ref, value_ref, ikey_ref, ivalue_ref = (
            (key0_ref, value0_ref, ikey0_ref, ivalue0_ref),
            (key1_ref, value1_ref, ikey1_ref, ivalue1_ref),
        )[block]
        pieces = (slice(0, BLOCK),) if block == 1 else (slice(0, TILE), slice(TILE, BLOCK))
        for piece in pieces:
            out = slice(block * BLOCK + piece.start, block * BLOCK + piece.stop)
            for head in range(heads):
                state = after_ref[head]
                if block == 0:
                    state = factor_of(table_ref, 1, heads, head) * state + second_ref[head]
                high, low = split(state)
                place = block * heads + head
                weight = column(table_ref[2, place : place + 1, piece])
                far_key = halves(nt(value_ref[piece, lanes(head)], jnp.concatenate([high, low], axis=0)))
                far_value = halves(nn(key_ref[piece, lanes(head)], jnp.concatenate([high, low], axis=1)))
                gkey_ref[out, lanes(head)] = (
                    ikey_ref[piece, lanes(head)].astype(F32) + weight * far_key
                ).astype(BF16)
                gvalue_ref[out, lanes(head)] = (
                    ivalue_ref[piece, lanes(head)].astype(F32) + weight * far_value
                ).astype(BF16)
            at = pl.ds(out.start, out.stop - out.start)
            for source, target in ((gkey_ref, gkey_hbm), (gvalue_ref, gvalue_hbm)):
                stores.append(
                    pltpu.make_async_copy(source.at[at], target.at[at], sems.at[len(loads) + len(stores)])
                )
                stores[-1].start()
    for store in stores:
        store.wait()


def sizes():
    return lax.axis_size("ctx"), lax.axis_size("tp")


def exchange(values, axis):
    return lax.all_to_all(values, axis, 0, 0, tiled=True)


def local(query_rows, key_rows, value_rows, gate_logits, norm_gain, log_decay, offsets, cotangent):
    heads = log_decay.shape[0]
    tokens, width = query_rows.shape
    ctx, tp = sizes()
    features = float(tp * width)
    gain = norm_gain.reshape(1, width)
    slice_rows = heads * D_HEAD // ctx
    chunks = tokens // CHUNK
    near, far = (pl.BlockSpec(memory_space=space) for space in (pltpu.VMEM, pltpu.HBM))

    def vmem(dtype, *shape):
        return pltpu.VMEM(shape or (tokens, width), dtype)

    def hbm(dtype, *shape):
        return pltpu.HBM(shape or (tokens, width), dtype)

    full, full_low = vmem(F32), vmem(BF16)
    half, half_low = vmem(F32, BLOCK, width), vmem(BF16, BLOCK, width)
    states = (heads, D_HEAD, D_HEAD)
    sends = vmem(F32, ctx, slice_rows + PAD, D_HEAD)
    slices = vmem(F32, ctx, slice_rows, D_HEAD)
    table = vmem(F32, 4, 2 * heads, BLOCK)

    def call(body, name, in_specs, outs, scratch=(), copies=0, cost=1.0, aliases=None):
        if copies:
            scratch = (*scratch, pltpu.SemaphoreType.DMA((copies,)))
        made = pl.pallas_call(
            body,
            in_specs=in_specs,
            out_specs=[near if out.memory_space == pltpu.VMEM else far for out in outs],
            out_shape=outs,
            scratch_shapes=scratch,
            name=name,
            input_output_aliases=aliases or {},
            cost_estimate=pl.CostEstimate(
                flops=int(cost * 5e8), bytes_accessed=int(cost * 2e6), transcendentals=0
            ),
            compiler_params=pltpu.CompilerParams(vmem_limit_bytes=ROOM),
        )

        def pinned(*arrays):
            return made(
                *(
                    pltpu.with_memory_space_constraint(array, pltpu.VMEM if spec is near else pltpu.HBM)
                    for array, spec in zip(arrays, in_specs)
                )
            )

        return pinned

    tables, send, first = call(
        functools.partial(tables_kernel, heads),
        "tables",
        [far] * 4,
        [table, sends, hbm(F32, *states)],
        scratch=[full_low, full_low, vmem(F32, *states), vmem(F32, heads, tokens), pltpu.SMEM(offsets.shape, jnp.int32)],
        copies=7,
        cost=3,
    )(offsets, log_decay, key_rows, value_rows)

    def scan(backward, got, wait_for, where):
        return call(
            functools.partial(scan_kernel, backward), "scan", [near, where], [slices], cost=0.5
        )(got, wait_for)[0]

    got = exchange(send, "ctx")
    early, late = (heads, TILE, TILE), (heads, BLOCK, TILE)
    inner, early_weights, late_weights = call(
        functools.partial(inner_kernel, heads),
        "inner",
        [far, far, far, near],
        [full, hbm(BF16, *early), hbm(BF16, *late)],
        scratch=[full_low] * 3 + [vmem(BF16, *early), vmem(BF16, *late)],
        copies=8,
        cost=5,
    )(query_rows, key_rows, value_rows, tables)
    prefixes = scan(False, got, inner, near)
    before = exchange(prefixes, "ctx").reshape(states)
    (normgrad,) = call(
        gate_kernel,
        "gate",
        [far, far, near, near],
        [hbm(F32)],
        scratch=[full_low, full_low, full],
        copies=6,
        cost=4,
    )(gate_logits, cotangent, gain, prefixes)

    attention, stats, queries, normgrad_near, carry, gates = call(
        functools.partial(attention_kernel, heads),
        "attention",
        [far, far, far, far, near, near, near],
        [full, vmem(F32, tp, 2 * chunks, CHUNK), full_low, full, full, full_low],
        scratch=[vmem(F32, *states)],
        copies=6,
        cost=2,
    )(query_rows, normgrad, first, gate_logits, inner, before, tables)
    stats = exchange(stats, "tp")

    first_grad, second_grad, rest, send, second, attended, grad_gate = call(
        functools.partial(gradient_kernel, heads, features),
        "gradient",
        [near] * 8,
        [half_low, half_low, hbm(BF16), sends, hbm(F32, *states), hbm(BF16), hbm(BF16)],
        scratch=[full_low, full, vmem(F32, *states), full_low, full_low, full],
        copies=6,
        cost=3,
    )(gates, stats, attention, normgrad_near, queries, tables, carry, gain)
    got = exchange(send, "ctx")

    back_specs = [far] * 4 + [near] * 3
    sources = (query_rows, key_rows, value_rows, rest)
    half_hbm = hbm(BF16, BLOCK, width)
    grad_query, ikey0, ivalue0 = call(
        functools.partial(back_kernel, heads, 0),
        "back0",
        back_specs,
        [hbm(BF16), half_hbm, half_hbm],
        scratch=[half_low] * 7,
        copies=7,
        cost=5,
    )(*sources, first_grad, before, tables)
    suffixes = scan(True, got, grad_query, far)
    after = exchange(suffixes, "ctx").reshape(states)
    grad_query, ikey1, ivalue1, keys1, values1 = call(
        functools.partial(back_kernel, heads, 1),
        "back1",
        [*back_specs, far, far, far, near, far],
        [hbm(BF16), half_low, half_low, half_low, half_low],
        scratch=[vmem(F32, *states), vmem(BF16, *early), vmem(BF16, *late), half_low, half_low, half_low],
        copies=8,
        cost=5,
        aliases={11: 0},
    )(*sources, second_grad, before, tables, first, early_weights, late_weights, suffixes, grad_query)
    grad_key, grad_value = call(
        functools.partial(far_kernel, heads),
        "far",
        [far] * 5 + [near] * 6 + [far],
        [hbm(BF16)] * 2,
        scratch=[half_low] * 4 + [vmem(F32, *states), full_low, full_low],
        copies=11,
        cost=3,
    )(key_rows, value_rows, ikey0, ivalue0, second, ikey1, ivalue1, keys1, values1, after, tables, grad_query)
    return (attended, grad_query, grad_key, grad_value, grad_gate)


def solution(mesh):
    placed = (
        P("ctx", "tp"),
        P("ctx", "tp"),
        P("ctx", "tp"),
        P("ctx", "tp"),
        P("tp"),
        P("tp", "ctx"),
        P(),
        P("ctx", "tp"),
    )
    return jax.shard_map(
        local,
        mesh=mesh,
        in_specs=placed,
        out_specs=(P("ctx", "tp"), P("ctx", "tp"), P("ctx", "tp"), P("ctx", "tp"), P("ctx", "tp")),
        check_vma=False,
    )
```
